256 devices in a mesh: dp: 64 (over y, z, core), grp: 4 (over x).
Axes of the slice: x: 4, y: 4, z: 8, core: 2. Of those that a mesh axis runs over, the one named last changes fastest.
Arguments:
- params: float32 [64, 4, 256, 1024], P('dp', 'grp'), may hold values from -3 to 3
- momentum: float32 [64, 4, 256, 1024], P('dp', 'grp'), may hold values from -60 to 60
- variance: float32 [64, 4, 256, 1024], P('dp', 'grp'), may hold values from 0.1 to 2
- worker_error: float32 [64, 4, 256, 1024], P('dp', 'grp'), may hold values from -4 to 4
- grads: bfloat16 [64, 4, 256, 1024], P('dp', 'grp'), may hold values from -12 to 12
- server_error: float32 [256, 1024], P(('dp', 'grp')), may hold values from -1.5 to 1.5
- sync_rows: int32 [256], replicated, may hold values 0 or 1
- var_rows: int32 [256], replicated, may hold values 0 or 1
- step: int32 [1], replicated, may hold values from 0 to 1023
- lr_table: float32 [1024], replicated, may hold values from 0.02 to 0.5
Outputs:
- new_params: float32 [64, 4, 256, 1024], P('dp', 'grp')
- new_momentum: float32 [64, 4, 256, 1024], P('dp', 'grp')
- new_variance: float32 [64, 4, 256, 1024], P('dp', 'grp')
- new_worker_error: float32 [64, 4, 256, 1024], P('dp', 'grp')
- new_server_error: float32 [256, 1024], P(('dp', 'grp'))
The draws below stay inside these ranges and needn't reach their ends.
Inputs may be any that keep to these rules, and one draw needn't show every extreme that they name: sync_rows holds at least one 1.
All inputs are finite; a program needn't handle non-finite values. Where the reference program divides by a largest or mean magnitude, that divisor is 1e-20 or more.
Results may differ from the reference program's by a relative error of at most 0.0003.
Values sent between devices are 32-bit elements; how exact they have to be, the bound alone decides.
A program may use at most 64 MiB of HBM per device.

```python
import math
import jax
import jax.numpy as jnp
from jax import lax

D = 1024
ROWS = 256
STEPS = 1024
N_DP = 64
N_GRP = 4


def draw_momentum(key, part):
    first, second = jax.random.split(jax.random.fold_in(key, 11), 2)
    scale = jnp.exp(jax.random.uniform(first, (N_DP, N_GRP, ROWS, 1), jnp.float32, 0.0, math.log(10.0)))
    return jnp.clip(jax.random.normal(second, (N_DP, N_GRP, ROWS, D), jnp.float32), -6.0, 6.0) * scale


def place_ends(result, key, least, largest):
    place = [jax.random.randint(jax.random.fold_in(key, axis), (), 0, length) for axis, length in enumerate(result.shape)]
    widest = result.shape.index(max(result.shape))
    beside = place[:widest] + [(place[widest] + 1) % result.shape[widest]] + place[widest + 1:]
    return result.at[tuple(place)].set(least).at[tuple(beside)].set(largest)


def steps_of(key, extent, cuts, smallest, largest):
    level = 1.0
    for axis_at, shards_of in cuts:
        heights = jax.random.uniform(jax.random.fold_in(jax.random.fold_in(key, 6), axis_at), (shards_of,), jnp.float32, smallest / len(cuts), largest / len(cuts))
        level = level * jnp.repeat(jnp.exp(heights), extent[axis_at] // shards_of).reshape((-1,) + (1,) * (len(extent) - 1 - axis_at))
    return level


def centred(stream_key, shape, deviation, most, shards=(), dtype=jnp.bfloat16):
    gain = steps_of(stream_key, shape, shards, -0.22, 0.18) if shards else 1.0
    values = jax.random.normal(stream_key, shape, jnp.float32) * deviation * gain
    return jnp.minimum(jnp.maximum(values, -most), most).astype(dtype)


def setup_inputs(seed: int = 0) -> dict:
    key_of = jax.random.split(jax.random.key(seed), 11)
    return {
        "params": centred(key_of[0], (N_DP, N_GRP, ROWS, D), 0.5, 3.0, ((0, 64), (1, 4)), jnp.float32),
        "momentum": draw_momentum(jax.random.fold_in(key_of[10], 71), 0),
        "variance": jnp.clip(jnp.exp(math.log(2.0) - 2.9957323 * jax.random.uniform(key_of[2], (N_DP, N_GRP, ROWS, D), jnp.float32) ** steps_of(key_of[2], (N_DP, N_GRP, ROWS, D), ((0, 64), (1, 4)), -0.2, 0.2)), 0.1, 2.0),
        "worker_error": centred(key_of[3], (N_DP, N_GRP, ROWS, D), 0.5, 4.0, ((0, 64), (1, 4)), jnp.float32),
        "grads": centred(key_of[4], (N_DP, N_GRP, ROWS, D), 2.0, 12.0, ((0, 64), (1, 4))),
        "server_error": centred(key_of[5], (ROWS, D), 0.2, 1.5, ((0, 256),), jnp.float32),
        "sync_rows": place_ends((jax.random.randint(key_of[6], (ROWS,), 0, 4) < 3).astype(jnp.int32), jax.random.fold_in(key_of[6], 1), 0, 1),
        "var_rows": place_ends((jax.random.randint(key_of[7], (ROWS,), 0, 2) < 1).astype(jnp.int32), jax.random.fold_in(key_of[7], 1), 0, 1),
        "step": jax.random.randint(key_of[8], (1,), 0, STEPS).astype(jnp.int32),
        "lr_table": jnp.clip(jnp.exp(jax.random.uniform(key_of[9], (STEPS,), jnp.float32, math.log(0.02), math.log(0.5))), 0.02, 0.5),
    }


SATURATION = 0.25
BETA_ONE = 0.9
BETA_TWO = 0.95
EPS_SCALE = 1e-06
EPS_ADAM = 1e-08

def compress(values):
    scale = lax.optimization_barrier(jnp.mean(jnp.abs(values), axis=-1, keepdims=True)) + EPS_SCALE
    return (scale * jnp.clip(values / (SATURATION * scale), -1.0, 1.0), scale)

def reference(params, momentum, variance, worker_error, grads, server_error, sync_rows, var_rows, step, lr_table):
    gradient = grads.astype(jnp.float32)
    moment = BETA_ONE * momentum + (1.0 - BETA_ONE) * gradient
    compensated = moment + worker_error
    packed, unused = compress(compensated)
    synced_mask = (sync_rows == 1)[:, None]
    sent_terms = jnp.where(synced_mask, packed, 0.0)
    new_worker_error = jnp.where(synced_mask, compensated - sent_terms, worker_error)
    averaged = lax.optimization_barrier(jnp.sum(sent_terms, axis=(0, 1))) / jnp.float32(N_DP * N_GRP) + server_error
    synced, row_scale = compress(averaged)
    new_server_error = jnp.where(synced_mask, averaged - synced, server_error)
    new_momentum = jnp.where(synced_mask, synced, moment)
    square_sum = jnp.sum(jnp.where(sync_rows == 1, row_scale[:, 0] * row_scale[:, 0], 0.0))
    synced_count = jnp.sum(sync_rows).astype(jnp.float32)
    norm_factor = 1.0 / jnp.sqrt(square_sum / synced_count)
    new_variance = jnp.where((var_rows == 1)[:, None], BETA_TWO * variance + (1.0 - BETA_TWO) * gradient * gradient, variance)
    rate = lr_table[step[0]]
    new_params = params - rate * norm_factor * new_momentum / (jnp.sqrt(new_variance) + EPS_ADAM)
    return (new_params, new_momentum, new_variance, new_worker_error, new_server_error)
```

```python
import jax
import jax.numpy as jnp
from jax import lax
from jax.experimental import pallas as pl
from jax.experimental.pallas import tpu as pltpu
from jax.sharding import PartitionSpec as P

BETA_ONE = 0.9
BETA_TWO = 0.95
EPS_SCALE = 1e-06
EPS_ADAM = 1e-08
D = 1024
ROWS = 256
REPLICAS = 256
F32 = jnp.float32
OFFS = (2, 1, 3, 0)
BACK = {0: 0, 1: 2, 2: 1}
FAR_FIRST = (4, 3, 5, 2, 6, 1, 7)


def kernel(
    mom_h, we_h, g_h, var_h, par_h, se_v, sync_v, vrow_v, step_s, lr_s,
    npar, nmom, nvar, nwe, nse,
    mom_b, we_b, g_b, var_b, par_b, smask, vmask,
    sent, rp, r_far, r_left, r_right, r_b, r_z, t_mine, t_other, se_o, se_t, nse_t, zg, gath,
    ld, ps, pr, fs, fr, ls, lr, rs, rr, bs, br, zs, zr, ms, mr,
    gzs, gzr, gbs, gbr, gls, glr, grs, grr, gfs, gfr, gps, gpr,
):
    dp = lax.axis_index("dp")
    x = lax.axis_index("grp")
    c = dp % 2
    z = (dp // 2) % 8
    y = dp // 16

    def dev(xx, yy, zz, cc):
        return ((yy * 8 + zz) * 2 + cc, xx)

    def dev_a(k):
        return dev((x + (1 - c) * k) % 4, (y + c * k) % 4, z, c)

    def dev_b(k):
        return dev((x + c * k) % 4, (y + (1 - c) * k) % 4, z, c)

    def dev_z(k):
        return dev(x, y, (z + k) % 8, c)

    partner = dev(x, y, z, 1 - c)
    a = (1 - c) * x + c * y
    b = c * x + (1 - c) * y
    step_a = 4 - 3 * c
    step_b = 1 + 3 * c
    right, left, far = (a + 1) % 4, (a + 3) % 4, (a + 2) % 4
    cols = [(b + o) % 4 for o in OFFS]

    def chunk(A, i):
        return A * step_a + cols[i] * step_b

    def rdma(src, dst, ssem, rsem, device):
        return pltpu.make_async_remote_copy(
            src_ref=src, dst_ref=dst, send_sem=ssem, recv_sem=rsem,
            device_id=device, device_id_type=pl.DeviceIdType.MESH,
        )

    barrier = pltpu.get_barrier_semaphore()
    peers = [partner, dev_a(1), dev_a(3)]
    peers += [dev_b(k) for k in (1, 2, 3)]
    peers += [dev_z(k) for k in range(1, 8)]
    for peer in peers:
        pl.semaphore_signal(barrier, inc=1, device_id=peer, device_id_type=pl.DeviceIdType.MESH)

    y_of = [(y + o) % 4 for o in OFFS]
    loads = []
    for i in range(4):
        rows = pl.ds(pl.multiple_of(y_of[i] * 64, 64), 64)
        group = []
        for n, (src, dst) in enumerate(((mom_h, mom_b), (we_h, we_b), (g_h, g_b))):
            copy = pltpu.make_async_copy(src.at[rows], dst.at[rows], ld.at[i * 3 + n])
            copy.start()
            group.append(copy)
        loads.append(group)
    load_var = pltpu.make_async_copy(var_h, var_b, ld.at[12])
    load_par = pltpu.make_async_copy(par_h, par_b, ld.at[13])
    load_var.start()
    load_par.start()

    diagonal = lax.broadcasted_iota(jnp.int32, (128, 128), 0) == lax.broadcasted_iota(jnp.int32, (128, 128), 1)
    for source, mask in ((sync_v, smask), (vrow_v, vmask)):
        for k in range(2):
            line = jnp.where(source[k : k + 1, :] == 1, 1.0, 0.0).astype(F32)
            column = jnp.sum(jnp.where(diagonal, jnp.broadcast_to(line, (128, 128)), 0.0), axis=1, keepdims=True)
            mask[pl.ds(k * 128, 128), :] = jnp.broadcast_to(column, (128, 128))
    synced_count = jnp.sum(jnp.where(sync_v[...] == 1, 1.0, 0.0).astype(F32))

    pl.semaphore_wait(barrier, len(peers))

    se_copy = rdma(se_v, se_o, ms.at[1], mr.at[1], partner)
    se_copy.start()

    pair_copies = []
    for i in range(4):
        for copy in loads[i]:
            copy.wait()

        def rows16(q, carry, i=i):
            start = pl.multiple_of(y_of[i] * 64 + q * 16, 16)
            rows = pl.ds(start, 16)
            moment = BETA_ONE * mom_b[rows, :] + (1.0 - BETA_ONE) * g_b[rows, :].astype(F32)
            nmom[rows, :] = moment
            error = we_b[rows, :]
            comp = moment + error
            scale = jnp.sum(jnp.abs(comp), axis=1, keepdims=True) * (1.0 / D) + EPS_SCALE
            packed = jnp.minimum(jnp.maximum(4.0 * comp, -scale), scale)
            on = smask[rows, :][:, :1] > 0.5
            terms = jnp.where(on, packed, 0.0)
            nwe[rows, :] = jnp.where(on, comp - packed, error)
            for half in range(2):
                for j in range(4):
                    lanes = (half * 4 + j) * 128
                    for sub in range(4):
                        at = half * 1024 + y_of[i] * 64 + (q * 2 + sub // 2) * 8 + (sub % 2) * 4 + j
                        sent[pl.ds(at, 4, stride=256), :] = terms[sub * 4 : sub * 4 + 4, lanes : lanes + 128]
            return carry

        lax.fori_loop(0, 4, rows16, 0)
        for xx in range(4):
            at = xx * 4 + y_of[i]
            copy = rdma(
                sent.at[pl.ds(pl.multiple_of((1 - c) * 1024 + at * 64, 64), 64)],
                rp.at[pl.ds(pl.multiple_of(at * 64, 64), 64)],
                ps.at[at], pr.at[at], partner,
            )
            copy.start()
            pair_copies.append(copy)

    def part(A, i):
        return pl.ds(pl.multiple_of(c * 1024 + chunk(A, i) * 64, 64), 64)

    def pair(A, i):
        at = chunk(A, i)
        mine = pl.ds(pl.multiple_of(at * 64, 64), 64)
        pltpu.make_async_copy(rp.at[mine], rp.at[mine], pr.at[at]).wait()
        sent[part(A, i), :] += rp[mine, :]

    sends = []

    def send(src, dst, ssem, rsem, device):
        copy = rdma(src, dst, ssem, rsem, device)
        copy.start()
        sends.append(copy)
        return copy

    to_right, to_left = dev_a(1), dev_a(3)
    far_copies, left_copies, right_copies = {}, {}, {}
    for i in (0, 1):
        pair(far, i)
        far_copies[i] = send(sent.at[part(far, i)], r_far.at[i], fs.at[i], fr.at[i], to_right)
    for i in (2, 3):
        pair(far, i)
        far_copies[i] = send(sent.at[part(far, i)], r_far.at[i], fs.at[i], fr.at[i], to_left)
    for i in (2, 3):
        pair(right, i)
        left_copies[i] = send(sent.at[part(right, i)], r_left.at[i], ls.at[i], lr.at[i], to_right)
        pair(left, i - 2)
        right_copies[i - 2] = send(
            sent.at[part(left, i - 2)], r_right.at[i - 2], rs.at[i - 2], rr.at[i - 2], to_left
        )
    for i in (0, 1):
        pair(right, i)
        pair(left, i + 2)
    for i in range(4):
        pair(a, i)
    for i in (0, 1):
        far_copies[i].wait_recv()
        sent[part(right, i), :] += r_far[i]
        left_copies[i] = send(sent.at[part(right, i)], r_left.at[i], ls.at[i], lr.at[i], to_right)
        far_copies[i + 2].wait_recv()
        sent[part(left, i + 2), :] += r_far[i + 2]
        right_copies[i + 2] = send(
            sent.at[part(left, i + 2)], r_right.at[i + 2], rs.at[i + 2], rr.at[i + 2], to_left
        )
    b_copies = []
    for i in range(4):
        left_copies[i].wait_recv()
        right_copies[i].wait_recv()
        sent[part(a, i), :] += r_left[i] + r_right[i]
        if i < 3:
            b_copies.append(send(sent.at[part(a, i)], r_b.at[i], bs.at[i], br.at[i], dev_b(OFFS[i])))
    for copy in b_copies:
        copy.wait_recv()
    sent[part(a, 3), :] += (r_b[0] + r_b[1]) + r_b[2]
    own = c * 1024 + chunk(a, 3) * 64
    z_copies = []
    for k in FAR_FIRST:
        tile = pl.ds(pl.multiple_of(own + ((z + k) % 8) * 8, 8), 8)
        z_copies.append(send(sent.at[tile], r_z.at[k - 1], zs.at[k - 1], zr.at[k - 1], dev_z(k)))

    rate = lr_s[step_s[0]]
    load_var.wait()
    load_par.wait()

    def rows16v(q, carry):
        rows = pl.ds(pl.multiple_of(q * 16, 16), 16)
        g = g_b[rows, :].astype(F32)
        v = var_b[rows, :]
        on = vmask[rows, :][:, :1] > 0.5
        v = jnp.where(on, BETA_TWO * v + (1.0 - BETA_TWO) * g * g, v)
        nvar[rows, :] = v
        npar[rows, :] = rate / (jnp.sqrt(v) + EPS_ADAM)
        return carry

    lax.fori_loop(0, 16, rows16v, 0)
    se_copy.wait_recv()
    for half in range(2):
        for j in range(4):
            lanes = pl.ds((half * 4 + j) * 128, 128)
            se_t[pl.ds(half * 8 + c * 4 + j, 1), :] = se_v[:, lanes]
            se_t[pl.ds(half * 8 + (1 - c) * 4 + j, 1), :] = se_o[:, lanes]

    for copy in z_copies:
        copy.wait_recv()
    total = sent[pl.ds(pl.multiple_of(own + z * 8, 8), 8), :]
    for k in range(7):
        total = total + r_z[k]
    t_mine[...] = total
    swap = send(t_mine, t_other, ms.at[0], mr.at[0], partner)
    low = lax.broadcasted_iota(jnp.int32, (8, 128), 0) < 4
    average = total * (1.0 / REPLICAS) + se_t[pl.ds(pl.multiple_of(c * 8, 8), 8), :]
    swap.wait_recv()
    other = t_other[...] * (1.0 / REPLICAS) + se_t[pl.ds(pl.multiple_of((1 - c) * 8, 8), 8), :]
    absolute = jnp.abs(average) + jnp.abs(other)
    first = jnp.sum(jnp.where(low, absolute, 0.0)) * (1.0 / D) + EPS_SCALE
    second = jnp.sum(jnp.where(low, 0.0, absolute)) * (1.0 / D) + EPS_SCALE
    scale = jnp.where(low, first, second)
    synced = jnp.minimum(jnp.maximum(4.0 * average, -scale), scale)
    row = y * 64 + z * 8 + x
    on_first = smask[pl.ds(row, 1), :]
    on_second = smask[pl.ds(row + 4, 1), :]
    squares = on_first * (first * first) + on_second * (second * second)
    zg[z, 0:8, :] = synced
    zg[z, 8:16, :] = jnp.broadcast_to(squares, (8, 128))
    gz_copies = []
    for k in FAR_FIRST:
        gz_copies.append(send(zg.at[z], zg.at[z], gzs.at[k - 1], gzr.at[k - 1], dev_z(k)))

    synced_other = jnp.minimum(jnp.maximum(4.0 * other, -scale), scale)
    nse_t[pl.ds(pl.multiple_of(c * 8, 8), 8), :] = average - synced
    nse_t[pl.ds(pl.multiple_of((1 - c) * 8, 8), 8), :] = other - synced_other
    own_on = smask[pl.ds(row + 4 * c, 1), :] > 0.5
    for half in range(2):
        for j in range(4):
            lanes = pl.ds((half * 4 + j) * 128, 128)
            nse[:, lanes] = jnp.where(own_on, nse_t[pl.ds(half * 8 + c * 4 + j, 1), :], se_v[:, lanes])

    def block(half, at):
        return pl.ds(pl.multiple_of((half * 16 + at) * 72, 8), 72)

    for k in range(1, 8):
        came = zg.at[(z + 8 - k) % 8]
        pltpu.make_async_copy(came, came, gzr.at[k - 1]).wait()
    base = pl.multiple_of((c * 16 + chunk(a, 3)) * 72, 8)
    extra = zg[0, 8:16, :]
    for zz in range(8):
        gath[pl.ds(base + zz * 8, 8), :] = zg[zz, 0:8, :]
        if zz:
            extra = extra + zg[zz, 8:16, :]
    gath[pl.ds(base + 64, 8), :] = extra

    relays = []

    def share(A, i, n):
        at = gath.at[block(c, chunk(A, i))]
        relays.append(send(at, at, gps.at[n], gpr.at[n], partner))

    def forward(i):
        at = gath.at[block(c, chunk(a, i))]
        send(at, at, grs.at[i], grr.at[i], to_right)
        send(at, at, gls.at[i], glr.at[i], to_left)

    def arrived(A, i, sem):
        at = gath.at[block(c, chunk(A, i))]
        pltpu.make_async_copy(at, at, sem).wait()

    def pass_on(A, i, device):
        at = gath.at[block(c, chunk(A, i))]
        send(at, at, gfs.at[i], gfr.at[i], device)

    mine = gath.at[block(c, chunk(a, 3))]
    for i in range(3):
        send(mine, mine, gbs.at[i], gbr.at[i], dev_b(OFFS[i]))
    forward(3)
    share(a, 3, 3)
    for i in (1, 2, 0):
        arrived(a, i, gbr.at[BACK[i]])
        forward(i)
        share(a, i, i)
        if i == 2:
            arrived(left, 3, grr.at[3])
            pass_on(left, 3, to_right)
            share(left, 3, 7)
            arrived(right, 3, glr.at[3])
            share(right, 3, 11)
    for i in (1, 2, 0):
        arrived(right, i, glr.at[i])
        if i:
            pass_on(right, i, to_left)
        arrived(left, i, grr.at[i])
        if not i:
            pass_on(left, i, to_right)
        share(right, i, 8 + i)
        share(left, i, 4 + i)
    for i in (3, 1, 2, 0):
        arrived(far, i, gfr.at[i])
        share(far, i, 12 + i)
    for copy in relays:
        copy.wait_recv()

    squares = gath[pl.ds(pl.multiple_of(c * 1152 + 64, 8), 8), :]
    for n in range(1, 16):
        squares = squares + gath[pl.ds(pl.multiple_of(c * 1152 + n * 72 + 64, 8), 8), :]
    norm = 1.0 / jnp.sqrt(squares / synced_count)

    def finish(r, carry):
        rows = pl.ds(pl.multiple_of(r * 8, 8), 8)
        on = smask[rows, :] > 0.5
        at = (r // 8) * 72 + (r % 8) * 8
        for half in range(2):
            for j in range(4):
                lanes = pl.ds((half * 4 + j) * 128, 128)
                top = gath[pl.ds(half * 1152 + at + j, 4, stride=288), :]
                bottom = gath[pl.ds(half * 1152 + at + 4 + j, 4, stride=288), :]
                value = jnp.where(on, jnp.concatenate([top, bottom], axis=0), nmom[rows, lanes])
                nmom[rows, lanes] = value
                npar[rows, lanes] = par_b[rows, lanes] - norm * (npar[rows, lanes] * value)
        return carry

    lax.fori_loop(0, 32, finish, 0)

    for copy in pair_copies:
        copy.wait_send()
    se_copy.wait_send()
    for copy in sends:
        copy.wait_send()


def on_device(params, momentum, variance, worker_error, grads, server_error, sync_rows, var_rows, step, lr_table):
    flat = lambda v: v.reshape(ROWS, D)
    hbm = pl.BlockSpec(memory_space=pl.ANY)
    vmem = pl.BlockSpec(memory_space=pltpu.VMEM)
    smem = pl.BlockSpec(memory_space=pltpu.SMEM)
    full = jax.ShapeDtypeStruct((ROWS, D), F32)
    dma = pltpu.SemaphoreType.DMA
    outs = pl.pallas_call(
        kernel,
        out_shape=(full, full, full, full, jax.ShapeDtypeStruct((1, D), F32)),
        in_specs=[hbm] * 5 + [vmem] * 3 + [smem] * 2,
        out_specs=(vmem,) * 5,
        scratch_shapes=[
            pltpu.VMEM((ROWS, D), F32),
            pltpu.VMEM((ROWS, D), F32),
            pltpu.VMEM((ROWS, D), jnp.bfloat16),
            pltpu.VMEM((ROWS, D), F32),
            pltpu.VMEM((ROWS, D), F32),
            pltpu.VMEM((ROWS, 128), F32),
            pltpu.VMEM((ROWS, 128), F32),
            pltpu.VMEM((2048, 128), F32),
            pltpu.VMEM((1024, 128), F32),
            pltpu.VMEM((4, 64, 128), F32),
            pltpu.VMEM((4, 64, 128), F32),
            pltpu.VMEM((4, 64, 128), F32),
            pltpu.VMEM((3, 64, 128), F32),
            pltpu.VMEM((7, 8, 128), F32),
            pltpu.VMEM((8, 128), F32),
            pltpu.VMEM((8, 128), F32),
            pltpu.VMEM((1, D), F32),
            pltpu.VMEM((16, 128), F32),
            pltpu.VMEM((16, 128), F32),
            pltpu.VMEM((8, 16, 128), F32),
            pltpu.VMEM((2304, 128), F32),
            dma((14,)), dma((16,)), dma((16,)),
            dma((4,)), dma((4,)), dma((4,)), dma((4,)), dma((4,)), dma((4,)),
            dma((3,)), dma((3,)), dma((7,)), dma((7,)), dma((2,)), dma((2,)),
            dma((7,)), dma((7,)), dma((3,)), dma((3,)),
            dma((4,)), dma((4,)), dma((4,)), dma((4,)), dma((4,)), dma((4,)),
            dma((16,)), dma((16,)),
        ],
        compiler_params=pltpu.CompilerParams(
            collective_id=0, has_side_effects=True, vmem_limit_bytes=40 * 1024 * 1024
        ),
        name="momentum_exchange",
    )(
        flat(momentum), flat(worker_error), flat(grads), flat(variance), flat(params),
        server_error, sync_rows.reshape(2, 128), var_rows.reshape(2, 128), step, lr_table,
    )
    back = lambda v: v.reshape(1, 1, ROWS, D)
    return tuple(back(v) for v in outs[:4]) + (outs[4],)


def solution(mesh):
    big = P("dp", "grp", None, None)
    return jax.shard_map(
        on_device,
        mesh=mesh,
        in_specs=(big,) * 5 + (P(("dp", "grp"), None), P(), P(), P(), P()),
        out_specs=(big,) * 4 + (P(("dp", "grp"), None),),
        check_vma=False,
    )
```

```python
import jax
import jax.numpy as jnp
from jax import lax
from jax.experimental import pallas as pl
from jax.experimental.pallas import tpu as pltpu
from jax.sharding import PartitionSpec as P

BETA_ONE = 0.9
BETA_TWO = 0.95
EPS_SCALE = 1e-06
EPS_ADAM = 1e-08
D = 1024
ROWS = 256
REPLICAS = 256
F32 = jnp.float32
OFFS = (2, 1, 3, 0)
BACK = {0: 0, 1: 2, 2: 1}
FAR_FIRST = (4, 3, 5, 2, 6, 1, 7)


def kernel(
    mom_h, we_h, g_h, var_h, par_h, se_h, sync_h, vrow_h, lr_h, step_s,
    gath, nmom, npar, nvar, nwe, par_b, smask, norm_v, nse,
    mom_b, we_b, g_b, var_b, vmask, se_v, sync_v, vrow_v, lr_s,
    sent, rp, r_far, r_left, r_right, r_b, r_z, t_mine, t_other, se_o, se_t, nse_t, zg,
    ld, ps, pr, fs, fr, ls, lr, rs, rr, bs, br, zs, zr, ms, mr,
    gzs, gzr, gbs, gbr, gls, glr, grs, grr, gfs, gfr, gps, gpr,
):
    dp = lax.axis_index("dp")
    x = lax.axis_index("grp")
    c = dp % 2
    z = (dp // 2) % 8
    y = dp // 16

    def dev(xx, yy, zz, cc):
        return ((yy * 8 + zz) * 2 + cc, xx)

    def dev_a(k):
        return dev((x + (1 - c) * k) % 4, (y + c * k) % 4, z, c)

    def dev_b(k):
        return dev((x + c * k) % 4, (y + (1 - c) * k) % 4, z, c)

    def dev_z(k):
        return dev(x, y, (z + k) % 8, c)

    partner = dev(x, y, z, 1 - c)
    a = (1 - c) * x + c * y
    b = c * x + (1 - c) * y
    step_a = 4 - 3 * c
    step_b = 1 + 3 * c
    right, left, far = (a + 1) % 4, (a + 3) % 4, (a + 2) % 4
    cols = [(b + o) % 4 for o in OFFS]

    def chunk(A, i):
        return A * step_a + cols[i] * step_b

    def rdma(src, dst, ssem, rsem, device):
        return pltpu.make_async_remote_copy(
            src_ref=src, dst_ref=dst, send_sem=ssem, recv_sem=rsem,
            device_id=device, device_id_type=pl.DeviceIdType.MESH,
        )

    barrier = pltpu.get_barrier_semaphore()
    peers = [partner, dev_a(1), dev_a(3)]
    peers += [dev_b(k) for k in (1, 2, 3)]
    peers += [dev_z(k) for k in range(1, 8)]
    for peer in peers:
        pl.semaphore_signal(barrier, inc=1, device_id=peer, device_id_type=pl.DeviceIdType.MESH)

    small = []
    for n, (src, dst) in enumerate(
        ((sync_h, sync_v), (vrow_h, vrow_v), (se_h, se_v), (lr_h, lr_s))
    ):
        copy = pltpu.make_async_copy(src, dst, ld.at[14 + n])
        copy.start()
        small.append(copy)
    y_of = [(y + o) % 4 for o in OFFS]
    loads = []
    for i in range(4):
        rows = pl.ds(pl.multiple_of(y_of[i] * 64, 64), 64)
        group = []
        for n, (src, dst) in enumerate(((mom_h, mom_b), (we_h, we_b), (g_h, g_b))):
            copy = pltpu.make_async_copy(src.at[rows], dst.at[rows], ld.at[i * 3 + n])
            copy.start()
            group.append(copy)
        loads.append(group)
    load_var = pltpu.make_async_copy(var_h, var_b, ld.at[12])
    load_par = pltpu.make_async_copy(par_h, par_b, ld.at[13])
    load_var.start()
    load_par.start()

    for copy in small:
        copy.wait()

    diagonal = lax.broadcasted_iota(jnp.int32, (128, 128), 0) == lax.broadcasted_iota(jnp.int32, (128, 128), 1)
    for source, mask in ((sync_v, smask), (vrow_v, vmask)):
        for k in range(2):
            line = jnp.where(source[k : k + 1, :] == 1, 1.0, 0.0).astype(F32)
            column = jnp.sum(jnp.where(diagonal, jnp.broadcast_to(line, (128, 128)), 0.0), axis=1, keepdims=True)
            mask[pl.ds(k * 128, 128), :] = jnp.broadcast_to(column, (128, 128))
    synced_count = jnp.sum(jnp.where(sync_v[...] == 1, 1.0, 0.0).astype(F32))

    pl.semaphore_wait(barrier, len(peers))

    se_copy = rdma(se_v, se_o, ms.at[1], mr.at[1], partner)
    se_copy.start()

    pair_copies = []
    for i in range(4):
        for copy in loads[i]:
            copy.wait()

        def rows16(q, carry, i=i):
            start = pl.multiple_of(y_of[i] * 64 + q * 16, 16)
            rows = pl.ds(start, 16)
            moment = BETA_ONE * mom_b[rows, :] + (1.0 - BETA_ONE) * g_b[rows, :].astype(F32)
            nmom[rows, :] = moment
            error = we_b[rows, :]
            comp = moment + error
            scale = jnp.sum(jnp.abs(comp), axis=1, keepdims=True) * (1.0 / D) + EPS_SCALE
            packed = jnp.minimum(jnp.maximum(4.0 * comp, -scale), scale)
            on = smask[rows, :][:, :1] > 0.5
            terms = jnp.where(on, packed, 0.0)
            nwe[rows, :] = jnp.where(on, comp - packed, error)
            for half in range(2):
                for j in range(4):
                    lanes = (half * 4 + j) * 128
                    for sub in range(4):
                        at = half * 1024 + y_of[i] * 64 + (q * 2 + sub // 2) * 8 + (sub % 2) * 4 + j
                        sent[pl.ds(at, 4, stride=256), :] = terms[sub * 4 : sub * 4 + 4, lanes : lanes + 128]
            return carry

        lax.fori_loop(0, 4, rows16, 0)
        for xx in range(4):
            at = xx * 4 + y_of[i]
            copy = rdma(
                sent.at[pl.ds(pl.multiple_of((1 - c) * 1024 + at * 64, 64), 64)],
                rp.at[pl.ds(pl.multiple_of(at * 64, 64), 64)],
                ps.at[at], pr.at[at], partner,
            )
            copy.start()
            pair_copies.append(copy)

    def part(A, i):
        return pl.ds(pl.multiple_of(c * 1024 + chunk(A, i) * 64, 64), 64)

    def pair(A, i):
        at = chunk(A, i)
        mine = pl.ds(pl.multiple_of(at * 64, 64), 64)
        pltpu.make_async_copy(rp.at[mine], rp.at[mine], pr.at[at]).wait()
        sent[part(A, i), :] += rp[mine, :]

    sends = []

    def send(src, dst, ssem, rsem, device):
        copy = rdma(src, dst, ssem, rsem, device)
        copy.start()
        sends.append(copy)
        return copy

    to_right, to_left = dev_a(1), dev_a(3)
    far_copies, left_copies, right_copies = {}, {}, {}
    for i in (0, 1):
        pair(far, i)
        far_copies[i] = send(sent.at[part(far, i)], r_far.at[i], fs.at[i], fr.at[i], to_right)
    for i in (2, 3):
        pair(far, i)
        far_copies[i] = send(sent.at[part(far, i)], r_far.at[i], fs.at[i], fr.at[i], to_left)
    for i in (2, 3):
        pair(right, i)
        left_copies[i] = send(sent.at[part(right, i)], r_left.at[i], ls.at[i], lr.at[i], to_right)
        pair(left, i - 2)
        right_copies[i - 2] = send(
            sent.at[part(left, i - 2)], r_right.at[i - 2], rs.at[i - 2], rr.at[i - 2], to_left
        )
    for i in (0, 1):
        pair(right, i)
        pair(left, i + 2)
    for i in range(4):
        pair(a, i)
    for i in (0, 1):
        far_copies[i].wait_recv()
        sent[part(right, i), :] += r_far[i]
        left_copies[i] = send(sent.at[part(right, i)], r_left.at[i], ls.at[i], lr.at[i], to_right)
        far_copies[i + 2].wait_recv()
        sent[part(left, i + 2), :] += r_far[i + 2]
        right_copies[i + 2] = send(
            sent.at[part(left, i + 2)], r_right.at[i + 2], rs.at[i + 2], rr.at[i + 2], to_left
        )
    b_copies = []
    for i in range(4):
        left_copies[i].wait_recv()
        right_copies[i].wait_recv()
        sent[part(a, i), :] += r_left[i] + r_right[i]
        if i < 3:
            b_copies.append(send(sent.at[part(a, i)], r_b.at[i], bs.at[i], br.at[i], dev_b(OFFS[i])))
    for copy in b_copies:
        copy.wait_recv()
    sent[part(a, 3), :] += (r_b[0] + r_b[1]) + r_b[2]
    own = c * 1024 + chunk(a, 3) * 64
    z_copies = []
    for k in FAR_FIRST:
        tile = pl.ds(pl.multiple_of(own + ((z + k) % 8) * 8, 8), 8)
        z_copies.append(send(sent.at[tile], r_z.at[k - 1], zs.at[k - 1], zr.at[k - 1], dev_z(k)))

    rate = lr_s[step_s[0]]
    load_var.wait()
    load_par.wait()

    def rows16v(q, carry):
        rows = pl.ds(pl.multiple_of(q * 16, 16), 16)
        g = g_b[rows, :].astype(F32)
        v = var_b[rows, :]
        on = vmask[rows, :][:, :1] > 0.5
        v = jnp.where(on, BETA_TWO * v + (1.0 - BETA_TWO) * g * g, v)
        nvar[rows, :] = v
        npar[rows, :] = rate / (jnp.sqrt(v) + EPS_ADAM)
        return carry

    lax.fori_loop(0, 16, rows16v, 0)
    se_copy.wait_recv()
    for half in range(2):
        for j in range(4):
            lanes = pl.ds((half * 4 + j) * 128, 128)
            se_t[pl.ds(half * 8 + c * 4 + j, 1), :] = se_v[:, lanes]
            se_t[pl.ds(half * 8 + (1 - c) * 4 + j, 1), :] = se_o[:, lanes]

    for copy in z_copies:
        copy.wait_recv()
    total = sent[pl.ds(pl.multiple_of(own + z * 8, 8), 8), :]
    for k in range(7):
        total = total + r_z[k]
    t_mine[...] = total
    swap = send(t_mine, t_other, ms.at[0], mr.at[0], partner)
    low = lax.broadcasted_iota(jnp.int32, (8, 128), 0) < 4
    average = total * (1.0 / REPLICAS) + se_t[pl.ds(pl.multiple_of(c * 8, 8), 8), :]
    swap.wait_recv()
    other = t_other[...] * (1.0 / REPLICAS) + se_t[pl.ds(pl.multiple_of((1 - c) * 8, 8), 8), :]
    absolute = jnp.abs(average) + jnp.abs(other)
    first = jnp.sum(jnp.where(low, absolute, 0.0)) * (1.0 / D) + EPS_SCALE
    second = jnp.sum(jnp.where(low, 0.0, absolute)) * (1.0 / D) + EPS_SCALE
    scale = jnp.where(low, first, second)
    synced = jnp.minimum(jnp.maximum(4.0 * average, -scale), scale)
    row = y * 64 + z * 8 + x
    on_first = smask[pl.ds(row, 1), :]
    on_second = smask[pl.ds(row + 4, 1), :]
    squares = on_first * (first * first) + on_second * (second * second)
    zg[z, 0:8, :] = synced
    zg[z, 8:16, :] = jnp.broadcast_to(squares, (8, 128))
    gz_copies = []
    for k in FAR_FIRST:
        gz_copies.append(send(zg.at[z], zg.at[z], gzs.at[k - 1], gzr.at[k - 1], dev_z(k)))

    synced_other = jnp.minimum(jnp.maximum(4.0 * other, -scale), scale)
    nse_t[pl.ds(pl.multiple_of(c * 8, 8), 8), :] = average - synced
    nse_t[pl.ds(pl.multiple_of((1 - c) * 8, 8), 8), :] = other - synced_other
    own_on = smask[pl.ds(row + 4 * c, 1), :] > 0.5
    for half in range(2):
        for j in range(4):
            lanes = pl.ds((half * 4 + j) * 128, 128)
            nse[:, lanes] = jnp.where(own_on, nse_t[pl.ds(half * 8 + c * 4 + j, 1), :], se_v[:, lanes])

    def block(half, at):
        return pl.ds(pl.multiple_of((half * 16 + at) * 72, 8), 72)

    for k in range(1, 8):
        came = zg.at[(z + 8 - k) % 8]
        pltpu.make_async_copy(came, came, gzr.at[k - 1]).wait()
    base = pl.multiple_of((c * 16 + chunk(a, 3)) * 72, 8)
    extra = zg[0, 8:16, :]
    for zz in range(8):
        gath[pl.ds(base + zz * 8, 8), :] = zg[zz, 0:8, :]
        if zz:
            extra = extra + zg[zz, 8:16, :]
    gath[pl.ds(base + 64, 8), :] = extra

    relays = []

    def share(A, i, n):
        at = gath.at[block(c, chunk(A, i))]
        relays.append(send(at, at, gps.at[n], gpr.at[n], partner))

    def forward(i):
        at = gath.at[block(c, chunk(a, i))]
        send(at, at, grs.at[i], grr.at[i], to_right)
        send(at, at, gls.at[i], glr.at[i], to_left)

    def arrived(A, i, sem):
        at = gath.at[block(c, chunk(A, i))]
        pltpu.make_async_copy(at, at, sem).wait()

    def pass_on(A, i, device):
        at = gath.at[block(c, chunk(A, i))]
        send(at, at, gfs.at[i], gfr.at[i], device)

    mine = gath.at[block(c, chunk(a, 3))]
    for i in range(3):
        send(mine, mine, gbs.at[i], gbr.at[i], dev_b(OFFS[i]))
    forward(3)
    share(a, 3, 3)
    for i in (1, 2, 0):
        arrived(a, i, gbr.at[BACK[i]])
        forward(i)
        share(a, i, i)
        if i == 2:
            arrived(left, 3, grr.at[3])
            pass_on(left, 3, to_right)
            share(left, 3, 7)
            arrived(right, 3, glr.at[3])
            share(right, 3, 11)
    for i in (1, 2, 0):
        arrived(right, i, glr.at[i])
        if i:
            pass_on(right, i, to_left)
        arrived(left, i, grr.at[i])
        if not i:
            pass_on(left, i, to_right)
        share(right, i, 8 + i)
        share(left, i, 4 + i)
    for i in (3, 1, 2, 0):
        arrived(far, i, gfr.at[i])
        share(far, i, 12 + i)
    for copy in relays:
        copy.wait_recv()

    squares = gath[pl.ds(pl.multiple_of(c * 1152 + 64, 8), 8), :]
    for n in range(1, 16):
        squares = squares + gath[pl.ds(pl.multiple_of(c * 1152 + n * 72 + 64, 8), 8), :]
    norm = 1.0 / jnp.sqrt(squares / synced_count)

    norm_v[...] = norm

    for copy in pair_copies:
        copy.wait_send()
    se_copy.wait_send()
    for copy in sends:
        copy.wait_send()


def finish_kernel(
    gath, nmom, slope, nvar, nwe, par_b, smask, norm_v, nse,
    par_o, mom_o, var_o, we_o, se_out, value_b, param_b, sems,
):
    copies = []

    def write(src, dst, n):
        copy = pltpu.make_async_copy(src, dst, sems.at[n])
        copy.start()
        copies.append(copy)

    write(nvar, var_o, 0)
    write(nwe, we_o, 1)
    write(nse, se_out, 2)
    norm = norm_v[...]
    for y in range(4):

        def finish(z, carry, y=y):
            rows = pl.ds(pl.multiple_of(y * 64 + z * 8, 8), 8)
            on = smask[rows, :] > 0.5
            at = y * 72 + z * 8
            for half in range(2):
                for j in range(4):
                    lanes = pl.ds((half * 4 + j) * 128, 128)
                    top = gath[pl.ds(half * 1152 + at + j, 4, stride=288), :]
                    bottom = gath[pl.ds(half * 1152 + at + 4 + j, 4, stride=288), :]
                    value = jnp.where(on, jnp.concatenate([top, bottom], axis=0), nmom[rows, lanes])
                    value_b[rows, lanes] = value
                    param_b[rows, lanes] = par_b[rows, lanes] - norm * (slope[rows, lanes] * value)
            return carry

        lax.fori_loop(0, 8, finish, 0)
        rows = pl.ds(y * 64, 64)
        write(value_b.at[rows], mom_o.at[rows], 3 + y)
        write(param_b.at[rows], par_o.at[rows], 7 + y)
    for copy in copies:
        copy.wait()


def on_device(params, momentum, variance, worker_error, grads, server_error, sync_rows, var_rows, step, lr_table):
    in_hbm = lambda v: pltpu.with_memory_space_constraint(v, pltpu.HBM)
    flat = lambda v: in_hbm(v.reshape(ROWS, D))
    hbm = pl.BlockSpec(memory_space=pltpu.HBM)
    vmem = pl.BlockSpec(memory_space=pltpu.VMEM)
    full = jax.ShapeDtypeStruct((ROWS, D), F32)
    dma = pltpu.SemaphoreType.DMA
    one = jax.ShapeDtypeStruct((1, D), F32)
    middle = pl.pallas_call(
        kernel,
        out_shape=(
            jax.ShapeDtypeStruct((2304, 128), F32), full, full, full, full, full,
            jax.ShapeDtypeStruct((ROWS, 128), F32), jax.ShapeDtypeStruct((8, 128), F32), one,
        ),
        in_specs=[hbm] * 9 + [pl.BlockSpec(memory_space=pltpu.SMEM)],
        out_specs=(vmem,) * 9,
        scratch_shapes=[
            pltpu.VMEM((ROWS, D), F32),
            pltpu.VMEM((ROWS, D), F32),
            pltpu.VMEM((ROWS, D), jnp.bfloat16),
            pltpu.VMEM((ROWS, D), F32),
            pltpu.VMEM((ROWS, 128), F32),
            pltpu.VMEM((1, D), F32),
            pltpu.VMEM((2, 128), jnp.int32),
            pltpu.VMEM((2, 128), jnp.int32),
            pltpu.SMEM((1024,), F32),
            pltpu.VMEM((2048, 128), F32),
            pltpu.VMEM((1024, 128), F32),
            pltpu.VMEM((4, 64, 128), F32),
            pltpu.VMEM((4, 64, 128), F32),
            pltpu.VMEM((4, 64, 128), F32),
            pltpu.VMEM((3, 64, 128), F32),
            pltpu.VMEM((7, 8, 128), F32),
            pltpu.VMEM((8, 128), F32),
            pltpu.VMEM((8, 128), F32),
            pltpu.VMEM((1, D), F32),
            pltpu.VMEM((16, 128), F32),
            pltpu.VMEM((16, 128), F32),
            pltpu.VMEM((8, 16, 128), F32),
            dma((18,)), dma((16,)), dma((16,)),
            dma((4,)), dma((4,)), dma((4,)), dma((4,)), dma((4,)), dma((4,)),
            dma((3,)), dma((3,)), dma((7,)), dma((7,)), dma((2,)), dma((2,)),
            dma((7,)), dma((7,)), dma((3,)), dma((3,)),
            dma((4,)), dma((4,)), dma((4,)), dma((4,)), dma((4,)), dma((4,)),
            dma((16,)), dma((16,)),
        ],
        compiler_params=pltpu.CompilerParams(
            collective_id=0, has_side_effects=True, vmem_limit_bytes=40 * 1024 * 1024
        ),
        name="momentum_exchange",
    )(
        flat(momentum), flat(worker_error), flat(grads), flat(variance), flat(params),
        in_hbm(server_error), in_hbm(sync_rows.reshape(2, 128)), in_hbm(var_rows.reshape(2, 128)),
        in_hbm(lr_table), step,
    )
    outs = pl.pallas_call(
        finish_kernel,
        out_shape=(full, full, full, full, one),
        in_specs=[vmem] * 9,
        out_specs=(hbm,) * 5,
        scratch_shapes=[pltpu.VMEM((ROWS, D), F32), pltpu.VMEM((ROWS, D), F32), dma((11,))],
        compiler_params=pltpu.CompilerParams(vmem_limit_bytes=24 * 1024 * 1024),
        name="update_and_write",
    )(*middle)
    back = lambda v: v.reshape(1, 1, ROWS, D)
    return tuple(back(v) for v in outs[:4]) + (outs[4],)


def solution(mesh):
    big = P("dp", "grp", None, None)
    return jax.shard_map(
        on_device,
        mesh=mesh,
        in_specs=(big,) * 5 + (P(("dp", "grp"), None), P(), P(), P(), P()),
        out_specs=(big,) * 4 + (P(("dp", "grp"), None),),
        check_vma=False,
    )
```

```python
import jax
import jax.numpy as jnp
from jax import lax
from jax.experimental import pallas as pl
from jax.experimental.pallas import tpu as pltpu
from jax.sharding import PartitionSpec as P

BETA_ONE = 0.9
BETA_TWO = 0.95
EPS_SCALE = 1e-06
EPS_ADAM = 1e-08
D = 1024
ROWS = 256
REPLICAS = 256
F32 = jnp.float32
ORDER = (2, 1, 3, 0)
PLANE = [(i, j) for j in ORDER for i in ORDER if (i, j) != (0, 0)]
FAR_FIRST = (4, 3, 5, 2, 6, 1, 7)


def kernel(
    mom_h, we_h, g_h, var_h, par_h, se_h, sync_h, vrow_h, lr_h, step_s,
    gat_a, gat_b, nmom, npar, nvar, nwe, par_b, smask, norm_v, nse,
    mom_b, we_b, g_b, var_b, vmask, se_v, sync_v, vrow_v, lr_s,
    part_a, part_b, pair_a, pair_b, in_a, in_b, in_a2, in_b2, sum_t, se_t, nse_t, row_t, row_b, up_a, up_b,
    ld, pas, par_, pbs, pbr, as1, ar1, bs1, br1, as2, ar2, bs2, br2,
    as3, ar3, bs3, br3, as4, ar4, bs4, br4, ras, rar, rbs, rbr,
):
    dp = lax.axis_index("dp")
    x = lax.axis_index("grp")
    c = dp % 2
    z = (dp // 2) % 8
    y = dp // 16
    q = x * 4 + y

    def dev(xx, yy, zz, cc):
        return ((yy * 8 + zz) * 2 + cc, xx)

    def plane(p):
        return (x + p[0]) % 4, (y + p[1]) % 4

    def to_plane(p):
        xx, yy = plane(p)
        return dev(xx, yy, z, c)

    def to_z(k):
        return dev(x, y, (z + k) % 8, c)

    partner = dev(x, y, z, 1 - c)

    def rows_at(start, size, multiple=8):
        return pl.ds(pl.multiple_of(start, multiple), size)

    sends = []

    def send(src, dst, ssem, rsem, device):
        copy = pltpu.make_async_remote_copy(
            src_ref=src, dst_ref=dst, send_sem=ssem, recv_sem=rsem,
            device_id=device, device_id_type=pl.DeviceIdType.MESH,
        )
        copy.start()
        sends.append(copy)
        return copy

    def landed(dst, sem):
        pltpu.make_async_copy(dst, dst, sem).wait()

    barrier = pltpu.get_barrier_semaphore()
    peers = [partner] + [to_plane(p) for p in PLANE] + [to_z(k) for k in range(1, 8)]
    for peer in peers:
        pl.semaphore_signal(barrier, inc=1, device_id=peer, device_id_type=pl.DeviceIdType.MESH)

    small = []
    for n, (src, dst) in enumerate(((sync_h, sync_v), (vrow_h, vrow_v), (se_h, se_v), (lr_h, lr_s))):
        copy = pltpu.make_async_copy(src, dst, ld.at[14 + n])
        copy.start()
        small.append(copy)
    y_of = [(y + o) % 4 for o in ORDER]
    loads = []
    for i in range(4):
        rows = rows_at(y_of[i] * 64, 64, 64)
        group = []
        for n, (src, dst) in enumerate(((mom_h, mom_b), (we_h, we_b), (g_h, g_b))):
            copy = pltpu.make_async_copy(src.at[rows], dst.at[rows], ld.at[i * 3 + n])
            copy.start()
            group.append(copy)
        loads.append(group)
    load_var = pltpu.make_async_copy(var_h, var_b, ld.at[12])
    load_par = pltpu.make_async_copy(par_h, par_b, ld.at[13])
    load_var.start()
    load_par.start()

    for copy in small:
        copy.wait()

    diagonal = lax.broadcasted_iota(jnp.int32, (128, 128), 0) == lax.broadcasted_iota(jnp.int32, (128, 128), 1)
    for source, mask in ((sync_v, smask), (vrow_v, vmask)):
        for k in range(2):
            line = jnp.where(source[k : k + 1, :] == 1, 1.0, 0.0).astype(F32)
            column = jnp.sum(jnp.where(diagonal, jnp.broadcast_to(line, (128, 128)), 0.0), axis=1, keepdims=True)
            mask[pl.ds(k * 128, 128), :] = jnp.broadcast_to(column, (128, 128))
    synced_count = jnp.sum(jnp.where(sync_v[...] == 1, 1.0, 0.0).astype(F32))

    for i in range(4):
        for copy in loads[i]:
            copy.wait()

        def rows32(n, carry, i=i):
            start = y_of[i] * 64 + n * 32
            rows = rows_at(start, 32, 32)
            moment = BETA_ONE * mom_b[rows, :] + (1.0 - BETA_ONE) * g_b[rows, :].astype(F32)
            nmom[rows, :] = moment
            error = we_b[rows, :]
            comp = moment + error
            scale = jnp.sum(jnp.abs(comp), axis=1, keepdims=True) * (1.0 / D) + EPS_SCALE
            packed = jnp.minimum(jnp.maximum(4.0 * comp, -scale), scale)
            on = smask[rows, :][:, :1] > 0.5
            terms = jnp.where(on, packed, 0.0)
            nwe[rows, :] = jnp.where(on, comp - packed, error)
            for sub in range(8):
                zz = n * 4 + sub // 2
                half = sub % 2
                for j in range(8):
                    value = terms[sub * 4 : sub * 4 + 4, j * 128 : j * 128 + 128]
                    if j < 4:
                        part_a[pl.ds(half * 512 + y_of[i] * 32 + zz * 4 + j, 4, stride=128), :] = value
                    else:
                        part_b[pl.ds(half * 512 + zz * 64 + y_of[i] * 4 + j - 4, 4, stride=16), :] = value
            return carry

        lax.fori_loop(0, 2, rows32, 0)
        if i == 0:
            pl.semaphore_wait(barrier, len(peers))
        for xx in range(4):
            at = xx * 4 + y_of[i]
            send(
                part_a.at[rows_at((1 - c) * 512 + at * 32, 32, 32)], pair_a.at[rows_at(at * 32, 32, 32)],
                pas.at[at], par_.at[at], partner,
            )
    for k in FAR_FIRST + (0,):
        at = (z + k) % 8
        send(
            part_b.at[rows_at((1 - c) * 512 + at * 64, 64, 64)], pair_b.at[rows_at(at * 64, 64, 64)],
            pbs.at[at], pbr.at[at], partner,
        )

    def whole_a(at):
        mine = rows_at(at * 32, 32, 32)
        landed(pair_a.at[mine], par_.at[at])
        return part_a[rows_at(c * 512 + at * 32, 32, 32), :] + pair_a[mine, :]

    def whole_b(at):
        mine = rows_at(at * 64, 64, 64)
        landed(pair_b.at[mine], pbr.at[at])
        return part_b[rows_at(c * 512 + at * 64, 64, 64), :] + pair_b[mine, :]

    came_a, came_b = [], []
    for n, p in enumerate(PLANE):
        xx, yy = plane(p)
        at = xx * 4 + yy
        here = rows_at(c * 512 + at * 32, 32, 32)
        part_a[here, :] = whole_a(at)
        came_a.append(send(part_a.at[here], in_a.at[n], as1.at[n], ar1.at[n], to_plane(p)))
    for k in FAR_FIRST:
        at = (z + k) % 8
        here = rows_at(c * 512 + at * 64, 64, 64)
        part_b[here, :] = whole_b(at)
        came_b.append(send(part_b.at[here], in_b.at[k - 1], bs1.at[k - 1], br1.at[k - 1], to_z(k)))
    here_a = rows_at(c * 512 + q * 32, 32, 32)
    here_b = rows_at(c * 512 + z * 64, 64, 64)
    part_a[here_a, :] = whole_a(q)
    part_b[here_b, :] = whole_b(z)

    for j in range(8):
        se_t[j : j + 1, :] = se_v[:, j * 128 : j * 128 + 128]

    total = part_a[here_a, :]
    for n in range(15):
        came_a[n].wait_recv()
        total = total + in_a[n]
    part_a[here_a, :] = total
    came_a2, came_b2 = [], []
    for k in FAR_FIRST:
        at = (z + k) % 8
        tile = rows_at(c * 512 + q * 32 + (at // 2) * 8, 8)
        came_a2.append(send(part_a.at[tile], in_a2.at[k - 1], as2.at[k - 1], ar2.at[k - 1], to_z(k)))
    total = part_b[here_b, :]
    for n, k in enumerate(FAR_FIRST):
        came_b[n].wait_recv()
        total = total + in_b[k - 1]
    part_b[here_b, :] = total
    for n, p in enumerate(PLANE):
        xx, yy = plane(p)
        tile = rows_at(c * 512 + z * 64 + ((xx * 4 + yy) // 2) * 8, 8)
        came_b2.append(send(part_b.at[tile], in_b2.at[n], bs2.at[n], br2.at[n], to_plane(p)))

    rate = lr_s[step_s[0]]
    load_var.wait()
    load_par.wait()

    def rows16v(n, carry):
        rows = rows_at(n * 16, 16, 16)
        g = g_b[rows, :].astype(F32)
        v = var_b[rows, :]
        on = vmask[rows, :][:, :1] > 0.5
        v = jnp.where(on, BETA_TWO * v + (1.0 - BETA_TWO) * g * g, v)
        nvar[rows, :] = v
        npar[rows, :] = rate / (jnp.sqrt(v) + EPS_ADAM)
        return carry

    lax.fori_loop(0, 16, rows16v, 0)

    total = part_a[rows_at(c * 512 + q * 32 + (z // 2) * 8, 8), :]
    for n, k in enumerate(FAR_FIRST):
        came_a2[n].wait_recv()
        total = total + in_a2[k - 1]
    sum_t[0:8, :] = total
    total = part_b[rows_at(c * 512 + z * 64 + (q // 2) * 8, 8), :]
    for n in range(15):
        came_b2[n].wait_recv()
        total = total + in_b2[n]
    sum_t[8:16, :] = total
    total = jnp.concatenate(
        [sum_t[pl.ds((z % 2) * 4, 4), :], sum_t[pl.ds(8 + (q % 2) * 4, 4), :]], axis=0
    )

    average = total * (1.0 / REPLICAS) + se_t[...]
    scale = jnp.sum(jnp.abs(average)) * (1.0 / D) + EPS_SCALE
    synced = jnp.minimum(jnp.maximum(4.0 * average, -scale), scale)
    own_on = smask[pl.ds(y * 64 + z * 8 + c * 4 + x, 1), :]
    squares = jnp.broadcast_to(own_on * (scale * scale), (8, 128))
    low = lax.broadcasted_iota(jnp.int32, (8, 128), 0) < 4
    row_t[...] = synced
    row_b[...] = jnp.where(low, squares, synced)
    for k in FAR_FIRST:
        send(row_t, up_a.at[z], as3.at[k - 1], ar3.at[k - 1], to_z(k))
    for n, p in enumerate(PLANE):
        send(row_b, up_b.at[q], bs3.at[n], br3.at[n], to_plane(p))
    nse_t[...] = jnp.where(own_on > 0.5, average - synced, se_t[...])
    for j in range(8):
        nse[:, j * 128 : j * 128 + 128] = nse_t[j : j + 1, :]

    up_a[z] = synced
    up_b[q] = jnp.where(low, squares, synced)
    for k in FAR_FIRST:
        landed(up_a.at[(z + 8 - k) % 8], ar3.at[k - 1])
    mine_a = rows_at(c * 512 + q * 32, 32, 32)
    for zz in range(8):
        gat_a[pl.ds(c * 512 + q * 32 + zz * 4, 4), :] = up_a[zz, 0:4, :]
    for n, p in enumerate(PLANE):
        send(gat_a.at[mine_a], gat_a.at[mine_a], as4.at[n], ar4.at[n], to_plane(p))
    send(gat_a.at[mine_a], gat_a.at[mine_a], ras.at[15], rar.at[15], partner)
    for n, p in enumerate(PLANE):
        landed(up_b.at[((x + 4 - p[0]) % 4) * 4 + (y + 4 - p[1]) % 4], br3.at[n])
    mine_b = rows_at(c * 576 + z * 72, 72)
    extra = up_b[0, 0:4, :]
    for n in range(16):
        gat_b[pl.ds(c * 576 + z * 72 + n * 4, 4), :] = up_b[n, 4:8, :]
        if n:
            extra = extra + up_b[n, 0:4, :]
    gat_b[pl.ds(c * 576 + z * 72 + 64, 4), :] = extra
    gat_b[pl.ds(c * 576 + z * 72 + 68, 4), :] = extra
    for k in FAR_FIRST:
        send(gat_b.at[mine_b], gat_b.at[mine_b], bs4.at[k - 1], br4.at[k - 1], to_z(k))
    send(gat_b.at[mine_b], gat_b.at[mine_b], rbs.at[7], rbr.at[7], partner)

    shared = []
    for n, p in enumerate(PLANE):
        at = ((x + 4 - p[0]) % 4) * 4 + (y + 4 - p[1]) % 4
        ref = gat_a.at[rows_at(c * 512 + at * 32, 32, 32)]
        landed(ref, ar4.at[n])
        shared.append(send(ref, ref, ras.at[n], rar.at[n], partner))
    for k in FAR_FIRST:
        ref = gat_b.at[rows_at(c * 576 + ((z + 8 - k) % 8) * 72, 72)]
        landed(ref, br4.at[k - 1])
        shared.append(send(ref, ref, rbs.at[k - 1], rbr.at[k - 1], partner))
    landed(gat_a.at[rows_at((1 - c) * 512 + q * 32, 32, 32)], rar.at[15])
    landed(gat_b.at[rows_at((1 - c) * 576 + z * 72, 72)], rbr.at[7])
    for copy in shared:
        copy.wait_recv()

    squares = gat_b[pl.ds(64, 8), :]
    for n in range(1, 16):
        squares = squares + gat_b[pl.ds(n * 72 + 64, 8), :]
    norm_v[...] = 1.0 / jnp.sqrt(squares / synced_count)

    for copy in sends:
        copy.wait_send()


def finish_kernel(
    gat_a, gat_b, nmom, slope, nvar, nwe, par_b, smask, norm_v, nse,
    par_o, mom_o, var_o, we_o, se_out, value_b, param_b, sems,
):
    copies = []

    def write(src, dst, n):
        copy = pltpu.make_async_copy(src, dst, sems.at[n])
        copy.start()
        copies.append(copy)

    write(nvar, var_o, 0)
    write(nwe, we_o, 1)
    write(nse, se_out, 2)
    norm = norm_v[...]
    for y in range(4):

        def finish(z, carry, y=y):
            rows = pl.ds(pl.multiple_of(y * 64 + z * 8, 8), 8)
            on = smask[rows, :] > 0.5
            for j in range(8):
                lanes = pl.ds(j * 128, 128)
                if j < 4:
                    at = y * 32 + z * 4 + j
                    halves = [gat_a[pl.ds(half * 512 + at, 4, stride=128), :] for half in range(2)]
                else:
                    at = z * 72 + y * 4 + j - 4
                    halves = [gat_b[pl.ds(half * 576 + at, 4, stride=16), :] for half in range(2)]
                value = jnp.where(on, jnp.concatenate(halves, axis=0), nmom[rows, lanes])
                value_b[rows, lanes] = value
                param_b[rows, lanes] = par_b[rows, lanes] - norm * (slope[rows, lanes] * value)
            return carry

        lax.fori_loop(0, 8, finish, 0)
        rows = pl.ds(y * 64, 64)
        write(value_b.at[rows], mom_o.at[rows], 3 + y)
        write(param_b.at[rows], par_o.at[rows], 7 + y)
    for copy in copies:
        copy.wait()


def on_device(params, momentum, variance, worker_error, grads, server_error, sync_rows, var_rows, step, lr_table):
    in_hbm = lambda v: pltpu.with_memory_space_constraint(v, pltpu.HBM)
    flat = lambda v: in_hbm(v.reshape(ROWS, D))
    hbm = pl.BlockSpec(memory_space=pltpu.HBM)
    vmem = pl.BlockSpec(memory_space=pltpu.VMEM)
    full = jax.ShapeDtypeStruct((ROWS, D), F32)
    dma = pltpu.SemaphoreType.DMA
    one = jax.ShapeDtypeStruct((1, D), F32)
    middle = pl.pallas_call(
        kernel,
        out_shape=(
            jax.ShapeDtypeStruct((1024, 128), F32), jax.ShapeDtypeStruct((1152, 128), F32),
            full, full, full, full, full,
            jax.ShapeDtypeStruct((ROWS, 128), F32), jax.ShapeDtypeStruct((8, 128), F32), one,
        ),
        in_specs=[hbm] * 9 + [pl.BlockSpec(memory_space=pltpu.SMEM)],
        out_specs=(vmem,) * 10,
        scratch_shapes=[
            pltpu.VMEM((ROWS, D), F32),
            pltpu.VMEM((ROWS, D), F32),
            pltpu.VMEM((ROWS, D), jnp.bfloat16),
            pltpu.VMEM((ROWS, D), F32),
            pltpu.VMEM((ROWS, 128), F32),
            pltpu.VMEM((1, D), F32),
            pltpu.VMEM((2, 128), jnp.int32),
            pltpu.VMEM((2, 128), jnp.int32),
            pltpu.SMEM((1024,), F32),
            pltpu.VMEM((1024, 128), F32),
            pltpu.VMEM((1024, 128), F32),
            pltpu.VMEM((512, 128), F32),
            pltpu.VMEM((512, 128), F32),
            pltpu.VMEM((15, 32, 128), F32),
            pltpu.VMEM((7, 64, 128), F32),
            pltpu.VMEM((7, 8, 128), F32),
            pltpu.VMEM((15, 8, 128), F32),
            pltpu.VMEM((16, 128), F32),
            pltpu.VMEM((8, 128), F32),
            pltpu.VMEM((8, 128), F32),
            pltpu.VMEM((8, 128), F32),
            pltpu.VMEM((8, 128), F32),
            pltpu.VMEM((8, 8, 128), F32),
            pltpu.VMEM((16, 8, 128), F32),
            dma((18,)), dma((16,)), dma((16,)), dma((8,)), dma((8,)),
            dma((15,)), dma((15,)), dma((7,)), dma((7,)),
            dma((7,)), dma((7,)), dma((15,)), dma((15,)),
            dma((7,)), dma((7,)), dma((15,)), dma((15,)),
            dma((15,)), dma((15,)), dma((7,)), dma((7,)),
            dma((16,)), dma((16,)), dma((8,)), dma((8,)),
        ],
        compiler_params=pltpu.CompilerParams(
            collective_id=0, has_side_effects=True, vmem_limit_bytes=40 * 1024 * 1024
        ),
        name="momentum_exchange",
    )(
        flat(momentum), flat(worker_error), flat(grads), flat(variance), flat(params),
        in_hbm(server_error), in_hbm(sync_rows.reshape(2, 128)), in_hbm(var_rows.reshape(2, 128)),
        in_hbm(lr_table), step,
    )
    outs = pl.pallas_call(
        finish_kernel,
        out_shape=(full, full, full, full, one),
        in_specs=[vmem] * 10,
        out_specs=(hbm,) * 5,
        scratch_shapes=[pltpu.VMEM((ROWS, D), F32), pltpu.VMEM((ROWS, D), F32), dma((11,))],
        compiler_params=pltpu.CompilerParams(vmem_limit_bytes=24 * 1024 * 1024),
        name="update_and_write",
    )(*middle)
    back = lambda v: v.reshape(1, 1, ROWS, D)
    return tuple(back(v) for v in outs[:4]) + (outs[4],)


def solution(mesh):
    big = P("dp", "grp", None, None)
    return jax.shard_map(
        on_device,
        mesh=mesh,
        in_specs=(big,) * 5 + (P(("dp", "grp"), None), P(), P(), P(), P()),
        out_specs=(big,) * 4 + (P(("dp", "grp"), None),),
        check_vma=False,
    )
```

```python
import jax
import jax.numpy as jnp
from jax import lax
from jax.experimental import pallas as pl
from jax.experimental.pallas import tpu as pltpu
from jax.sharding import PartitionSpec as P

BETA_ONE = 0.9
BETA_TWO = 0.95
EPS_SCALE = 1e-06
EPS_ADAM = 1e-08
D = 1024
ROWS = 256
REPLICAS = 256
F32 = jnp.float32
ORDER = (2, 1, 3, 0)
PLANE = [(i, j) for j in ORDER for i in ORDER if (i, j) != (0, 0)]
FAR_FIRST = (4, 3, 5, 2, 6, 1, 7)
GROUPS_A = [range(n, n + 3) for n in (0, 3, 6, 9, 12)]
GROUPS_B = [range(0, 3), range(3, 5), range(5, 7)]


def kernel(
    mom_h, we_h, g_h, var_h, par_h, se_h, sync_h, vrow_h, lr_h, step_s,
    gat_a, gat_b, nmom, npar, nvar, nwe, par_b, smask, norm_v, nse,
    mom_b, we_b, g_b, var_b, vmask, se_v, sync_v, vrow_v, lr_s,
    part_a, part_b, pair_a, pair_b, in_a, in_b, sum_a, out_a2, in_a2, in_b2, row_t, row_b, se_t, nse_t,
    up_a, up_b, s_in, s_mine, s_other,
    ld, out_sem, pair_sem, one, two, up_one, s_sem, up_two_a, up_two_b, share_sem,
):
    dp = lax.axis_index("dp")
    x = lax.axis_index("grp")
    c = dp % 2
    z = (dp // 2) % 8
    y = dp // 16
    q = x * 4 + y

    def rows_at(start, size, multiple=8):
        return pl.ds(pl.multiple_of(start, multiple), size)

    def drain(ref, sem):
        pltpu.make_async_copy(ref, ref, sem).wait()

    y_of = [(y + o) % 4 for o in ORDER]
    small = []
    for n, (src, dst) in enumerate(((sync_h, sync_v), (vrow_h, vrow_v), (se_h, se_v), (lr_h, lr_s))):
        small.append(pltpu.make_async_copy(src, dst, ld.at[n]))
    small[0].start()
    for i in range(4):
        rows = rows_at(y_of[i] * 64, 64, 64)
        for src, dst in ((mom_h, mom_b), (we_h, we_b), (g_h, g_b)):
            pltpu.make_async_copy(src.at[rows], dst.at[rows], ld.at[4 + i]).start()
    for copy in small[1:]:
        copy.start()

    def dev(xx, yy, zz, cc):
        return ((yy * 8 + zz) * 2 + cc, xx)

    def plane(p):
        return (x + p[0]) % 4, (y + p[1]) % 4

    def to_plane(p):
        xx, yy = plane(p)
        return dev(xx, yy, z, c)

    def to_z(k):
        return dev(x, y, (z + k) % 8, c)

    partner = dev(x, y, z, 1 - c)

    def send(src, dst, ssem, rsem, device):
        pltpu.make_async_remote_copy(
            src_ref=src, dst_ref=dst, send_sem=ssem, recv_sem=rsem,
            device_id=device, device_id_type=pl.DeviceIdType.MESH,
        ).start()

    barrier = pltpu.get_barrier_semaphore()
    peers = [to_z(k) for k in FAR_FIRST] + [to_plane(p) for p in PLANE] + [partner]
    for peer in peers:
        pl.semaphore_signal(barrier, inc=1, device_id=peer, device_id_type=pl.DeviceIdType.MESH)

    diagonal = lax.broadcasted_iota(jnp.int32, (128, 128), 0) == lax.broadcasted_iota(jnp.int32, (128, 128), 1)

    def spread(source, mask):
        for k in range(2):
            line = jnp.where(source[k : k + 1, :] == 1, 1.0, 0.0).astype(F32)
            column = jnp.sum(jnp.where(diagonal, jnp.broadcast_to(line, (128, 128)), 0.0), axis=1, keepdims=True)
            mask[pl.ds(k * 128, 128), :] = jnp.broadcast_to(column, (128, 128))

    small[0].wait()
    spread(sync_v, smask)

    for i in range(4):
        drain(mom_b.at[pl.ds(0, 160)], ld.at[4 + i])

        def rows32(n, carry, i=i):
            rows = rows_at(y_of[i] * 64 + n * 32, 32, 32)
            moment = BETA_ONE * mom_b[rows, :] + (1.0 - BETA_ONE) * g_b[rows, :].astype(F32)
            nmom[rows, :] = moment
            error = we_b[rows, :]
            comp = moment + error
            scale = jnp.sum(jnp.abs(comp), axis=1, keepdims=True) * (1.0 / D) + EPS_SCALE
            packed = jnp.minimum(jnp.maximum(4.0 * comp, -scale), scale)
            on = smask[rows, :][:, :1] > 0.5
            terms = jnp.where(on, packed, 0.0)
            nwe[rows, :] = jnp.where(on, comp - packed, error)
            for sub in range(8):
                zz = n * 4 + sub // 2
                half = sub % 2
                for j in range(8):
                    value = terms[sub * 4 : sub * 4 + 4, j * 128 : j * 128 + 128]
                    if j < 6:
                        part_a[pl.ds(half * 768 + y_of[i] * 48 + j * 8 + zz, 4, stride=192), :] = value
                    else:
                        part_b[pl.ds(half * 256 + zz * 32 + y_of[i] * 2 + j - 6, 4, stride=8), :] = value
            return carry

        lax.fori_loop(0, 2, rows32, 0)
        if i == 0:
            pl.semaphore_wait(barrier, len(peers))
        for xx in range(4):
            at = (xx * 4 + y_of[i]) * 48
            send(
                part_a.at[rows_at((1 - c) * 768 + at, 48)], pair_a.at[rows_at(at, 48)],
                out_sem.at[0], pair_sem.at[i], partner,
            )
    send(part_b.at[rows_at((1 - c) * 256, 256)], pair_b, out_sem.at[0], pair_sem.at[4], partner)
    load_var = pltpu.make_async_copy(var_h, var_b, ld.at[8])
    load_par = pltpu.make_async_copy(par_h, par_b, ld.at[9])
    load_var.start()
    load_par.start()

    n = 0
    for i in range(4):
        drain(pair_a.at[pl.ds(0, 192)], pair_sem.at[i])
        for dx in ORDER:
            p = (dx, ORDER[i])
            xx, yy = plane(p)
            at = (xx * 4 + yy) * 48
            here = rows_at(c * 768 + at, 48)
            part_a[here, :] += pair_a[rows_at(at, 48), :]
            if p != (0, 0):
                send(part_a.at[here], in_a.at[n], out_sem.at[1], one.at[0], to_plane(p))
                n += 1
    drain(pair_b, pair_sem.at[4])
    for k in FAR_FIRST + (0,):
        at = ((z + k) % 8) * 32
        here = rows_at(c * 256 + at, 32)
        part_b[here, :] += pair_b[rows_at(at, 32), :]
        if k:
            send(part_b.at[here], in_b.at[k - 1], out_sem.at[1], one.at[1], to_z(k))

    small[2].wait()
    for j in range(8):
        se_t[j : j + 1, :] = se_v[:, j * 128 : j * 128 + 128]

    drain(in_a, one.at[0])
    total = part_a[rows_at(c * 768 + q * 48, 48), :]
    for n in range(15):
        total = total + in_a[n]
    sum_a[...] = total
    for zz in range(8):
        out_a2[zz, 0:6, :] = sum_a[pl.ds(zz, 6, stride=8), :]
    for k in FAR_FIRST:
        send(out_a2.at[(z + k) % 8], in_a2.at[k - 1], out_sem.at[2], two.at[0], to_z(k))
    drain(in_b, one.at[1])
    here_b = rows_at(c * 256 + z * 32, 32)
    total = part_b[here_b, :]
    for n in range(7):
        total = total + in_b[n]
    part_b[here_b, :] = total
    for n, p in enumerate(PLANE):
        xx, yy = plane(p)
        tile = rows_at(c * 256 + z * 32 + ((xx * 4 + yy) // 4) * 8, 8)
        send(part_b.at[tile], in_b2.at[n], out_sem.at[2], two.at[1], to_plane(p))

    small[1].wait()
    small[3].wait()
    spread(vrow_v, vmask)
    rate = lr_s[step_s[0]]
    load_var.wait()
    load_par.wait()

    def rows16v(n, carry):
        rows = rows_at(n * 16, 16, 16)
        g = g_b[rows, :].astype(F32)
        v = var_b[rows, :]
        on = vmask[rows, :][:, :1] > 0.5
        v = jnp.where(on, BETA_TWO * v + (1.0 - BETA_TWO) * g * g, v)
        nvar[rows, :] = v
        npar[rows, :] = rate / (jnp.sqrt(v) + EPS_ADAM)
        return carry

    lax.fori_loop(0, 16, rows16v, 0)

    drain(in_a2, two.at[0])
    total = out_a2[z]
    for n in range(7):
        total = total + in_a2[n]
    row_t[...] = total
    drain(in_b2, two.at[1])
    total = part_b[rows_at(c * 256 + z * 32 + (q // 4) * 8, 8), :]
    for n in range(15):
        total = total + in_b2[n]
    row_b[...] = total
    row_t[6:8, :] = row_b[pl.ds((q % 4) * 2, 2), :]

    average = row_t[...] * (1.0 / REPLICAS) + se_t[...]
    scale = jnp.sum(jnp.abs(average)) * (1.0 / D) + EPS_SCALE
    synced = jnp.minimum(jnp.maximum(4.0 * average, -scale), scale)
    own_on = smask[pl.ds(y * 64 + z * 8 + c * 4 + x, 1), :]
    squares = jnp.broadcast_to(own_on * (scale * scale), (8, 128))
    mixed = jnp.where(lax.broadcasted_iota(jnp.int32, (8, 128), 0) < 6, squares, synced)
    row_t[...] = synced
    row_b[...] = mixed
    for k in FAR_FIRST:
        send(row_t, up_a.at[z], out_sem.at[3], up_one.at[0], to_z(k))
    for p in PLANE:
        send(row_b, up_b.at[q], out_sem.at[3], up_one.at[1], to_plane(p))
    nse_t[...] = jnp.where(own_on > 0.5, average - synced, se_t[...])
    for j in range(8):
        nse[:, j * 128 : j * 128 + 128] = nse_t[j : j + 1, :]
    synced_count = jnp.sum(jnp.where(sync_v[...] == 1, 1.0, 0.0).astype(F32))

    up_a[z] = synced
    up_b[q] = mixed
    drain(in_a2, up_one.at[0])
    mine_a = rows_at(c * 768 + q * 48, 48)
    for zz in range(8):
        gat_a[pl.ds(c * 768 + q * 48 + zz, 6, stride=8), :] = up_a[zz, 0:6, :]
    for n, group in enumerate(GROUPS_A):
        for m in group:
            send(gat_a.at[mine_a], gat_a.at[mine_a], out_sem.at[4], up_two_a.at[n], to_plane(PLANE[m]))
    send(gat_a.at[mine_a], gat_a.at[mine_a], out_sem.at[5], share_sem, partner)
    drain(in_b2, up_one.at[1])
    mine_b = rows_at(c * 256 + z * 32, 32)
    part = up_b[0, 0:1, :]
    for n in range(16):
        gat_b[pl.ds(c * 256 + z * 32 + n * 2, 2), :] = up_b[n, 6:8, :]
        if n:
            part = part + up_b[n, 0:1, :]
    for n, group in enumerate(GROUPS_B):
        for m in group:
            send(gat_b.at[mine_b], gat_b.at[mine_b], out_sem.at[4], up_two_b.at[n], to_z(FAR_FIRST[m]))
    send(gat_b.at[mine_b], gat_b.at[mine_b], out_sem.at[5], share_sem, partner)
    s_in[z] = part
    s_mine[...] = part
    for k in FAR_FIRST:
        send(s_mine, s_in.at[z], out_sem.at[6], s_sem.at[0], to_z(k))

    def share_a(group, n):
        drain(gat_a.at[pl.ds(0, 48 * len(group))], up_two_a.at[n])
        for m in group:
            p = PLANE[m]
            ref = gat_a.at[rows_at(c * 768 + (((x + 4 - p[0]) % 4) * 4 + (y + 4 - p[1]) % 4) * 48, 48)]
            send(ref, ref, out_sem.at[5], share_sem, partner)

    def share_b(group, n):
        drain(gat_b.at[pl.ds(0, 32 * len(group))], up_two_b.at[n])
        for m in group:
            ref = gat_b.at[rows_at(c * 256 + ((z + 8 - FAR_FIRST[m]) % 8) * 32, 32)]
            send(ref, ref, out_sem.at[5], share_sem, partner)

    share_a(GROUPS_A[0], 0)
    share_a(GROUPS_A[1], 1)
    share_b(GROUPS_B[0], 0)
    share_a(GROUPS_A[2], 2)
    share_b(GROUPS_B[1], 1)
    share_a(GROUPS_A[3], 3)
    share_b(GROUPS_B[2], 2)
    share_a(GROUPS_A[4], 4)

    drain(s_in.at[pl.ds(0, 7)], s_sem.at[0])
    part = s_in[0]
    for zz in range(1, 8):
        part = part + s_in[zz]
    s_in[8] = part
    send(s_in.at[8], s_other, out_sem.at[6], s_sem.at[1], partner)
    drain(s_other, s_sem.at[1])
    norm_v[...] = jnp.broadcast_to(1.0 / jnp.sqrt((part + s_other[...]) / synced_count), (8, 128))
    drain(gat_a.at[pl.ds(0, 1024)], share_sem)

    drain(gat_a.at[pl.ds(0, 1024)], out_sem.at[0])
    drain(gat_a.at[pl.ds(0, 944)], out_sem.at[1])
    drain(gat_a.at[pl.ds(0, 176)], out_sem.at[2])
    drain(gat_a.at[pl.ds(0, 176)], out_sem.at[3])
    drain(gat_a.at[pl.ds(0, 944)], out_sem.at[4])
    drain(gat_a.at[pl.ds(0, 1024)], out_sem.at[5])
    drain(s_in.at[pl.ds(0, 8)], out_sem.at[6])


def finish_kernel(
    gat_a, gat_b, nmom, slope, nvar, nwe, par_b, smask, norm_v, nse,
    par_o, mom_o, var_o, we_o, se_out, value_b, param_b, sems,
):
    copies = []

    def write(src, dst, n):
        copy = pltpu.make_async_copy(src, dst, sems.at[n])
        copy.start()
        copies.append(copy)

    write(nvar, var_o, 0)
    write(nwe, we_o, 1)
    write(nse, se_out, 2)
    norm = norm_v[...]
    for y in range(4):

        def finish(z, carry, y=y):
            rows = pl.ds(pl.multiple_of(y * 64 + z * 8, 8), 8)
            on = smask[rows, :] > 0.5
            for j in range(8):
                lanes = pl.ds(j * 128, 128)
                if j < 6:
                    at = y * 48 + j * 8 + z
                    halves = [gat_a[pl.ds(half * 768 + at, 4, stride=192), :] for half in range(2)]
                else:
                    at = z * 32 + y * 2 + j - 6
                    halves = [gat_b[pl.ds(half * 256 + at, 4, stride=8), :] for half in range(2)]
                value = jnp.where(on, jnp.concatenate(halves, axis=0), nmom[rows, lanes])
                value_b[rows, lanes] = value
                param_b[rows, lanes] = par_b[rows, lanes] - norm * (slope[rows, lanes] * value)
            return carry

        lax.fori_loop(0, 8, finish, 0)
        rows = pl.ds(y * 64, 64)
        write(value_b.at[rows], mom_o.at[rows], 3 + y)
        write(param_b.at[rows], par_o.at[rows], 7 + y)
    for copy in copies:
        copy.wait()


def on_device(params, momentum, variance, worker_error, grads, server_error, sync_rows, var_rows, step, lr_table):
    in_hbm = lambda v: pltpu.with_memory_space_constraint(v, pltpu.HBM)
    flat = lambda v: in_hbm(v.reshape(ROWS, D))
    hbm = pl.BlockSpec(memory_space=pltpu.HBM)
    vmem = pl.BlockSpec(memory_space=pltpu.VMEM)
    full = jax.ShapeDtypeStruct((ROWS, D), F32)
    dma = pltpu.SemaphoreType.DMA
    one = jax.ShapeDtypeStruct((1, D), F32)
    middle = pl.pallas_call(
        kernel,
        out_shape=(
            jax.ShapeDtypeStruct((1536, 128), F32), jax.ShapeDtypeStruct((512, 128), F32),
            full, full, full, full, full,
            jax.ShapeDtypeStruct((ROWS, 128), F32), jax.ShapeDtypeStruct((8, 128), F32), one,
        ),
        in_specs=[hbm] * 9 + [pl.BlockSpec(memory_space=pltpu.SMEM)],
        out_specs=(vmem,) * 10,
        scratch_shapes=[
            pltpu.VMEM((ROWS, D), F32),
            pltpu.VMEM((ROWS, D), F32),
            pltpu.VMEM((ROWS, D), jnp.bfloat16),
            pltpu.VMEM((ROWS, D), F32),
            pltpu.VMEM((ROWS, 128), F32),
            pltpu.VMEM((1, D), F32),
            pltpu.VMEM((2, 128), jnp.int32),
            pltpu.VMEM((2, 128), jnp.int32),
            pltpu.SMEM((1024,), F32),
            pltpu.VMEM((1536, 128), F32),
            pltpu.VMEM((512, 128), F32),
            pltpu.VMEM((768, 128), F32),
            pltpu.VMEM((256, 128), F32),
            pltpu.VMEM((15, 48, 128), F32),
            pltpu.VMEM((7, 32, 128), F32),
            pltpu.VMEM((48, 128), F32),
            pltpu.VMEM((8, 8, 128), F32),
            pltpu.VMEM((7, 8, 128), F32),
            pltpu.VMEM((15, 8, 128), F32),
            pltpu.VMEM((8, 128), F32),
            pltpu.VMEM((8, 128), F32),
            pltpu.VMEM((8, 128), F32),
            pltpu.VMEM((8, 128), F32),
            pltpu.VMEM((8, 8, 128), F32),
            pltpu.VMEM((16, 8, 128), F32),
            pltpu.VMEM((9, 1, 128), F32),
            pltpu.VMEM((1, 128), F32),
            pltpu.VMEM((1, 128), F32),
            dma((10,)), dma((7,)), dma((5,)), dma((2,)), dma((2,)), dma((2,)), dma((2,)),
            dma((5,)), dma((3,)), dma,
        ],
        compiler_params=pltpu.CompilerParams(
            collective_id=0, has_side_effects=True, vmem_limit_bytes=40 * 1024 * 1024
        ),
        name="momentum_exchange",
    )(
        flat(momentum), flat(worker_error), flat(grads), flat(variance), flat(params),
        in_hbm(server_error), in_hbm(sync_rows.reshape(2, 128)), in_hbm(var_rows.reshape(2, 128)),
        in_hbm(lr_table), step,
    )
    outs = pl.pallas_call(
        finish_kernel,
        out_shape=(full, full, full, full, one),
        in_specs=[vmem] * 10,
        out_specs=(hbm,) * 5,
        scratch_shapes=[pltpu.VMEM((ROWS, D), F32), pltpu.VMEM((ROWS, D), F32), dma((11,))],
        compiler_params=pltpu.CompilerParams(vmem_limit_bytes=24 * 1024 * 1024),
        name="update_and_write",
    )(*middle)
    back = lambda v: v.reshape(1, 1, ROWS, D)
    return tuple(back(v) for v in outs[:4]) + (outs[4],)


def solution(mesh):
    big = P("dp", "grp", None, None)
    return jax.shard_map(
        on_device,
        mesh=mesh,
        in_specs=(big,) * 5 + (P(("dp", "grp"), None), P(), P(), P(), P()),
        out_specs=(big,) * 4 + (P(("dp", "grp"), None),),
        check_vma=False,
    )
```

```python
import jax
import jax.numpy as jnp
from jax import lax
from jax.experimental import pallas as pl
from jax.experimental.pallas import tpu as pltpu
from jax.sharding import PartitionSpec as P

BETA_ONE = 0.9
BETA_TWO = 0.95
EPS_SCALE = 1e-06
EPS_ADAM = 1e-08
D = 1024
ROWS = 256
REPLICAS = 256
F32 = jnp.float32
ORDER = (2, 1, 3, 0)
PLANE = [(i, j) for j in ORDER for i in ORDER if (i, j) != (0, 0)]
FAR_FIRST = (4, 3, 5, 2, 6, 1, 7)
GROUPS_A = [range(n, n + 3) for n in (0, 3, 6, 9, 12)]
GROUPS_B = [range(0, 3), range(3, 5), range(5, 7)]


def kernel(
    mom_h, we_h, g_h, var_h, par_h, se_h, sync_h, vrow_h, lr_h, step_s,
    gat_a, gat_b, nmom, npar, nvar, nwe, par_b, smask, norm_v, nse,
    mom_b, we_b, g_b, var_b, vmask, se_v, sync_v, vrow_v, lr_s,
    part_a, part_b, pair_a, pair_b, in_a, in_b, sum_a, out_a2, in_a2, out_b2, in_b2, row_t, row_b, se_t, nse_t,
    up_a, up_b, s_in, s_mine, s_other,
    ld, out_sem, pair_sem, one, two, up_one, s_sem, up_two_a, up_two_b, share_sem,
):
    dp = lax.axis_index("dp")
    x = lax.axis_index("grp")
    c = dp % 2
    z = (dp // 2) % 8
    y = dp // 16
    q = x * 4 + y

    def rows_at(start, size, multiple=8):
        return pl.ds(pl.multiple_of(start, multiple), size)

    def drain(ref, sem):
        pltpu.make_async_copy(ref, ref, sem).wait()

    y_of = [(y + o) % 4 for o in ORDER]
    small = []
    for n, (src, dst) in enumerate(((sync_h, sync_v), (vrow_h, vrow_v), (se_h, se_v), (lr_h, lr_s))):
        small.append(pltpu.make_async_copy(src, dst, ld.at[n]))
    small[0].start()
    for i in range(4):
        rows = rows_at(y_of[i] * 64, 64, 64)
        for src, dst in ((mom_h, mom_b), (we_h, we_b), (g_h, g_b)):
            pltpu.make_async_copy(src.at[rows], dst.at[rows], ld.at[4 + i]).start()
    for copy in small[1:]:
        copy.start()

    def dev(xx, yy, zz, cc):
        return ((yy * 8 + zz) * 2 + cc, xx)

    def plane(p):
        return (x + p[0]) % 4, (y + p[1]) % 4

    def to_plane(p):
        xx, yy = plane(p)
        return dev(xx, yy, z, c)

    def to_z(k):
        return dev(x, y, (z + k) % 8, c)

    partner = dev(x, y, z, 1 - c)

    def send(src, dst, ssem, rsem, device):
        pltpu.make_async_remote_copy(
            src_ref=src, dst_ref=dst, send_sem=ssem, recv_sem=rsem,
            device_id=device, device_id_type=pl.DeviceIdType.MESH,
        ).start()

    barrier = pltpu.get_barrier_semaphore()
    peers = [to_z(k) for k in FAR_FIRST] + [to_plane(p) for p in PLANE] + [partner]
    for peer in peers:
        pl.semaphore_signal(barrier, inc=1, device_id=peer, device_id_type=pl.DeviceIdType.MESH)

    diagonal = lax.broadcasted_iota(jnp.int32, (128, 128), 0) == lax.broadcasted_iota(jnp.int32, (128, 128), 1)

    def spread(source, mask):
        for k in range(2):
            line = jnp.where(source[k : k + 1, :] == 1, 1.0, 0.0).astype(F32)
            column = jnp.sum(jnp.where(diagonal, jnp.broadcast_to(line, (128, 128)), 0.0), axis=1, keepdims=True)
            mask[pl.ds(k * 128, 128), :] = jnp.broadcast_to(column, (128, 128))

    small[0].wait()
    spread(sync_v, smask)

    for i in range(4):
        drain(mom_b.at[pl.ds(0, 160)], ld.at[4 + i])

        def rows32(n, carry, i=i):
            rows = rows_at(y_of[i] * 64 + n * 32, 32, 32)
            moment = BETA_ONE * mom_b[rows, :] + (1.0 - BETA_ONE) * g_b[rows, :].astype(F32)
            nmom[rows, :] = moment
            error = we_b[rows, :]
            comp = moment + error
            scale = jnp.sum(jnp.abs(comp), axis=1, keepdims=True) * (1.0 / D) + EPS_SCALE
            packed = jnp.minimum(jnp.maximum(4.0 * comp, -scale), scale)
            on = smask[rows, :][:, :1] > 0.5
            terms = jnp.where(on, packed, 0.0)
            nwe[rows, :] = jnp.where(on, comp - packed, error)
            for sub in range(8):
                zz = n * 4 + sub // 2
                half = sub % 2
                for j in range(8):
                    value = terms[sub * 4 : sub * 4 + 4, j * 128 : j * 128 + 128]
                    if j < 6:
                        part_a[pl.ds(half * 768 + y_of[i] * 48 + j * 8 + zz, 4, stride=192), :] = value
                    else:
                        part_b[pl.ds(half * 256 + zz * 32 + y_of[i] * 2 + j - 6, 4, stride=8), :] = value
            return carry

        lax.fori_loop(0, 2, rows32, 0)
    pl.semaphore_wait(barrier, len(peers))
    for i in range(4):
        for xx in range(4):
            at = (xx * 4 + y_of[i]) * 48
            send(
                part_a.at[rows_at((1 - c) * 768 + at, 48)], pair_a.at[rows_at(at, 48)],
                out_sem.at[0], pair_sem.at[i], partner,
            )
    send(part_b.at[rows_at((1 - c) * 256, 256)], pair_b, out_sem.at[0], pair_sem.at[4], partner)
    load_var = pltpu.make_async_copy(var_h, var_b, ld.at[8])
    load_par = pltpu.make_async_copy(par_h, par_b, ld.at[9])
    load_var.start()
    load_par.start()

    n = 0
    for i in range(4):
        drain(pair_a.at[pl.ds(0, 192)], pair_sem.at[i])
        for dx in ORDER:
            p = (dx, ORDER[i])
            xx, yy = plane(p)
            at = (xx * 4 + yy) * 48
            here = rows_at(c * 768 + at, 48)
            part_a[here, :] += pair_a[rows_at(at, 48), :]
            if p != (0, 0):
                send(part_a.at[here], in_a.at[n], out_sem.at[1], one.at[0], to_plane(p))
                n += 1
    drain(pair_b, pair_sem.at[4])
    for k in FAR_FIRST + (0,):
        at = ((z + k) % 8) * 32
        here = rows_at(c * 256 + at, 32)
        part_b[here, :] += pair_b[rows_at(at, 32), :]
        if k:
            send(part_b.at[here], in_b.at[k - 1], out_sem.at[1], one.at[1], to_z(k))

    small[2].wait()
    for j in range(8):
        se_t[j : j + 1, :] = se_v[:, j * 128 : j * 128 + 128]

    drain(in_a, one.at[0])
    total = part_a[rows_at(c * 768 + q * 48, 48), :]
    for n in range(15):
        total = total + in_a[n]
    sum_a[...] = total
    for zz in range(8):
        out_a2[zz, 0:6, :] = sum_a[pl.ds(zz, 6, stride=8), :]
    for k in FAR_FIRST:
        send(out_a2.at[(z + k) % 8], in_a2.at[k - 1], out_sem.at[2], two.at[0], to_z(k))
    drain(in_b, one.at[1])
    here_b = rows_at(c * 256 + z * 32, 32)
    total = part_b[here_b, :]
    for n in range(7):
        total = total + in_b[n]
    for n in range(16):
        out_b2[n] = total[n * 2 : n * 2 + 2, :]
    for n, p in enumerate(PLANE):
        xx, yy = plane(p)
        send(out_b2.at[xx * 4 + yy], in_b2.at[n], out_sem.at[7], two.at[1], to_plane(p))

    small[1].wait()
    small[3].wait()
    spread(vrow_v, vmask)
    rate = lr_s[step_s[0]]
    load_var.wait()
    load_par.wait()

    def rows16v(n, carry):
        rows = rows_at(n * 16, 16, 16)
        g = g_b[rows, :].astype(F32)
        v = var_b[rows, :]
        on = vmask[rows, :][:, :1] > 0.5
        v = jnp.where(on, BETA_TWO * v + (1.0 - BETA_TWO) * g * g, v)
        nvar[rows, :] = v
        npar[rows, :] = rate / (jnp.sqrt(v) + EPS_ADAM)
        return carry

    lax.fori_loop(0, 16, rows16v, 0)

    drain(in_a2, two.at[0])
    total = out_a2[z]
    for n in range(7):
        total = total + in_a2[n]
    row_t[...] = total
    drain(in_b2, two.at[1])
    total = out_b2[q]
    for n in range(15):
        total = total + in_b2[n]
    row_t[6:8, :] = total

    average = row_t[...] * (1.0 / REPLICAS) + se_t[...]
    scale = jnp.sum(jnp.abs(average)) * (1.0 / D) + EPS_SCALE
    synced = jnp.minimum(jnp.maximum(4.0 * average, -scale), scale)
    own_on = smask[pl.ds(y * 64 + z * 8 + c * 4 + x, 1), :]
    squares = jnp.broadcast_to(own_on * (scale * scale), (2, 128))
    row_t[...] = synced
    row_b[0:2, :] = synced[6:8, :]
    row_b[2:4, :] = squares
    for k in FAR_FIRST:
        send(row_t, up_a.at[z], out_sem.at[3], up_one.at[0], to_z(k))
    for p in PLANE:
        send(row_b, up_b.at[q], out_sem.at[8], up_one.at[1], to_plane(p))
    nse_t[...] = jnp.where(own_on > 0.5, average - synced, se_t[...])
    for j in range(8):
        nse[:, j * 128 : j * 128 + 128] = nse_t[j : j + 1, :]
    synced_count = jnp.sum(jnp.where(sync_v[...] == 1, 1.0, 0.0).astype(F32))

    up_a[z] = synced
    up_b[q, 0:2, :] = synced[6:8, :]
    up_b[q, 2:4, :] = squares
    drain(in_a2, up_one.at[0])
    mine_a = rows_at(c * 768 + q * 48, 48)
    for zz in range(8):
        gat_a[pl.ds(c * 768 + q * 48 + zz, 6, stride=8), :] = up_a[zz, 0:6, :]
    for n, group in enumerate(GROUPS_A):
        for m in group:
            send(gat_a.at[mine_a], gat_a.at[mine_a], out_sem.at[4], up_two_a.at[n], to_plane(PLANE[m]))
    send(gat_a.at[mine_a], gat_a.at[mine_a], out_sem.at[5], share_sem, partner)
    drain(up_b.at[pl.ds(0, 15)], up_one.at[1])
    mine_b = rows_at(c * 256 + z * 32, 32)
    part = up_b[0, 2:3, :]
    for n in range(16):
        gat_b[pl.ds(c * 256 + z * 32 + n * 2, 2), :] = up_b[n, 0:2, :]
        if n:
            part = part + up_b[n, 2:3, :]
    s_in[z] = part
    s_mine[...] = part
    for k in FAR_FIRST:
        send(s_mine, s_in.at[z], out_sem.at[6], s_sem.at[0], to_z(k))
    for n, group in enumerate(GROUPS_B):
        for m in group:
            send(gat_b.at[mine_b], gat_b.at[mine_b], out_sem.at[4], up_two_b.at[n], to_z(FAR_FIRST[m]))
    send(gat_b.at[mine_b], gat_b.at[mine_b], out_sem.at[5], share_sem, partner)

    def share_a(group, n):
        drain(gat_a.at[pl.ds(0, 48 * len(group))], up_two_a.at[n])
        for m in group:
            p = PLANE[m]
            ref = gat_a.at[rows_at(c * 768 + (((x + 4 - p[0]) % 4) * 4 + (y + 4 - p[1]) % 4) * 48, 48)]
            send(ref, ref, out_sem.at[5], share_sem, partner)

    def share_b(group, n):
        drain(gat_b.at[pl.ds(0, 32 * len(group))], up_two_b.at[n])
        for m in group:
            ref = gat_b.at[rows_at(c * 256 + ((z + 8 - FAR_FIRST[m]) % 8) * 32, 32)]
            send(ref, ref, out_sem.at[5], share_sem, partner)

    share_a(GROUPS_A[0], 0)
    share_a(GROUPS_A[1], 1)
    share_b(GROUPS_B[0], 0)
    share_a(GROUPS_A[2], 2)
    share_b(GROUPS_B[1], 1)
    share_a(GROUPS_A[3], 3)
    share_b(GROUPS_B[2], 2)
    share_a(GROUPS_A[4], 4)

    drain(s_in.at[pl.ds(0, 7)], s_sem.at[0])
    part = s_in[0]
    for zz in range(1, 8):
        part = part + s_in[zz]
    s_in[8] = part
    send(s_in.at[8], s_other, out_sem.at[6], s_sem.at[1], partner)
    drain(s_other, s_sem.at[1])
    norm_v[...] = jnp.broadcast_to(1.0 / jnp.sqrt((part + s_other[...]) / synced_count), (8, 128))
    drain(gat_a.at[pl.ds(0, 1024)], share_sem)

    drain(gat_a.at[pl.ds(0, 1024)], out_sem.at[0])
    drain(gat_a.at[pl.ds(0, 944)], out_sem.at[1])
    drain(in_a2, out_sem.at[2])
    drain(in_b2, out_sem.at[7])
    drain(in_a2, out_sem.at[3])
    drain(up_b.at[pl.ds(0, 15)], out_sem.at[8])
    drain(gat_a.at[pl.ds(0, 944)], out_sem.at[4])
    drain(gat_a.at[pl.ds(0, 1024)], out_sem.at[5])
    drain(s_in.at[pl.ds(0, 8)], out_sem.at[6])


def finish_kernel(
    gat_a, gat_b, nmom, slope, nvar, nwe, par_b, smask, norm_v, nse,
    par_o, mom_o, var_o, we_o, se_out, value_b, param_b, sems,
):
    copies = []

    def write(src, dst, n):
        copy = pltpu.make_async_copy(src, dst, sems.at[n])
        copy.start()
        copies.append(copy)

    write(nvar, var_o, 0)
    write(nwe, we_o, 1)
    write(nse, se_out, 2)
    norm = norm_v[...]
    for y in range(4):

        def finish(z, carry, y=y):
            rows = pl.ds(pl.multiple_of(y * 64 + z * 8, 8), 8)
            on = smask[rows, :] > 0.5
            for j in range(8):
                lanes = pl.ds(j * 128, 128)
                if j < 6:
                    at = y * 48 + j * 8 + z
                    halves = [gat_a[pl.ds(half * 768 + at, 4, stride=192), :] for half in range(2)]
                else:
                    at = z * 32 + y * 2 + j - 6
                    halves = [gat_b[pl.ds(half * 256 + at, 4, stride=8), :] for half in range(2)]
                value = jnp.where(on, jnp.concatenate(halves, axis=0), nmom[rows, lanes])
                value_b[rows, lanes] = value
                param_b[rows, lanes] = par_b[rows, lanes] - norm * (slope[rows, lanes] * value)
            return carry

        lax.fori_loop(0, 8, finish, 0)
        rows = pl.ds(y * 64, 64)
        write(value_b.at[rows], mom_o.at[rows], 3 + y)
        write(param_b.at[rows], par_o.at[rows], 7 + y)
    for copy in copies:
        copy.wait()


def on_device(params, momentum, variance, worker_error, grads, server_error, sync_rows, var_rows, step, lr_table):
    in_hbm = lambda v: pltpu.with_memory_space_constraint(v, pltpu.HBM)
    flat = lambda v: in_hbm(v.reshape(ROWS, D))
    hbm = pl.BlockSpec(memory_space=pltpu.HBM)
    vmem = pl.BlockSpec(memory_space=pltpu.VMEM)
    full = jax.ShapeDtypeStruct((ROWS, D), F32)
    dma = pltpu.SemaphoreType.DMA
    one = jax.ShapeDtypeStruct((1, D), F32)
    middle = pl.pallas_call(
        kernel,
        out_shape=(
            jax.ShapeDtypeStruct((1536, 128), F32), jax.ShapeDtypeStruct((512, 128), F32),
            full, full, full, full, full,
            jax.ShapeDtypeStruct((ROWS, 128), F32), jax.ShapeDtypeStruct((8, 128), F32), one,
        ),
        in_specs=[hbm] * 9 + [pl.BlockSpec(memory_space=pltpu.SMEM)],
        out_specs=(vmem,) * 10,
        scratch_shapes=[
            pltpu.VMEM((ROWS, D), F32),
            pltpu.VMEM((ROWS, D), F32),
            pltpu.VMEM((ROWS, D), jnp.bfloat16),
            pltpu.VMEM((ROWS, D), F32),
            pltpu.VMEM((ROWS, 128), F32),
            pltpu.VMEM((1, D), F32),
            pltpu.VMEM((2, 128), jnp.int32),
            pltpu.VMEM((2, 128), jnp.int32),
            pltpu.SMEM((1024,), F32),
            pltpu.VMEM((1536, 128), F32),
            pltpu.VMEM((512, 128), F32),
            pltpu.VMEM((768, 128), F32),
            pltpu.VMEM((256, 128), F32),
            pltpu.VMEM((15, 48, 128), F32),
            pltpu.VMEM((7, 32, 128), F32),
            pltpu.VMEM((48, 128), F32),
            pltpu.VMEM((8, 8, 128), F32),
            pltpu.VMEM((7, 8, 128), F32),
            pltpu.VMEM((16, 2, 128), F32),
            pltpu.VMEM((15, 2, 128), F32),
            pltpu.VMEM((8, 128), F32),
            pltpu.VMEM((4, 128), F32),
            pltpu.VMEM((8, 128), F32),
            pltpu.VMEM((8, 128), F32),
            pltpu.VMEM((8, 8, 128), F32),
            pltpu.VMEM((16, 4, 128), F32),
            pltpu.VMEM((9, 1, 128), F32),
            pltpu.VMEM((1, 128), F32),
            pltpu.VMEM((1, 128), F32),
            dma((10,)), dma((9,)), dma((5,)), dma((2,)), dma((2,)), dma((2,)), dma((2,)),
            dma((5,)), dma((3,)), dma,
        ],
        compiler_params=pltpu.CompilerParams(
            collective_id=0, has_side_effects=True, vmem_limit_bytes=40 * 1024 * 1024
        ),
        name="momentum_exchange",
    )(
        flat(momentum), flat(worker_error), flat(grads), flat(variance), flat(params),
        in_hbm(server_error), in_hbm(sync_rows.reshape(2, 128)), in_hbm(var_rows.reshape(2, 128)),
        in_hbm(lr_table), step,
    )
    outs = pl.pallas_call(
        finish_kernel,
        out_shape=(full, full, full, full, one),
        in_specs=[vmem] * 10,
        out_specs=(hbm,) * 5,
        scratch_shapes=[pltpu.VMEM((ROWS, D), F32), pltpu.VMEM((ROWS, D), F32), dma((11,))],
        compiler_params=pltpu.CompilerParams(vmem_limit_bytes=24 * 1024 * 1024),
        name="update_and_write",
    )(*middle)
    back = lambda v: v.reshape(1, 1, ROWS, D)
    return tuple(back(v) for v in outs[:4]) + (outs[4],)


def solution(mesh):
    big = P("dp", "grp", None, None)
    return jax.shard_map(
        on_device,
        mesh=mesh,
        in_specs=(big,) * 5 + (P(("dp", "grp"), None), P(), P(), P(), P()),
        out_specs=(big,) * 4 + (P(("dp", "grp"), None),),
        check_vma=False,
    )
```

```python
import jax
import jax.numpy as jnp
from jax import lax
from jax.experimental import pallas as pl
from jax.experimental.pallas import tpu as pltpu
from jax.sharding import PartitionSpec as P

BETA_ONE = 0.9
BETA_TWO = 0.95
EPS_SCALE = 1e-06
EPS_ADAM = 1e-08
D = 1024
ROWS = 256
REPLICAS = 256
F32 = jnp.float32
ORDER = (2, 1, 3, 0)
PLANE = [(i, j) for j in ORDER for i in ORDER if (i, j) != (0, 0)]
FAR_FIRST = (4, 3, 5, 2, 6, 1, 7)
GROUPS_A = [range(n, n + 5) for n in (0, 5, 10)]
GROUPS_B = [range(0, 4), range(4, 7)]


def kernel(
    mom_h, we_h, g_h, var_h, par_h, se_h, sync_h, vrow_h, lr_h, step_s,
    gat_a, gat_b, nmom, npar, nvar, nwe, par_b, smask, norm_v, nse,
    mom_b, we_b, g_b, var_b, vmask, se_v, sync_v, vrow_v, lr_s,
    part_a, part_b, pair_a, pair_b, in_a, in_b, sum_a, out_a2, in_a2, out_b2, in_b2, row_t, row_b, se_t, nse_t,
    up_a, up_b, s_in, s_mine, s_other,
    ld, out_sem, pair_sem, one, two, up_one, s_sem, up_two_a, up_two_b, share_sem,
):
    dp = lax.axis_index("dp")
    x = lax.axis_index("grp")
    c = dp % 2
    z = (dp // 2) % 8
    y = dp // 16
    q = x * 4 + y

    def rows_at(start, size, multiple=8):
        return pl.ds(pl.multiple_of(start, multiple), size)

    def drain(ref, sem):
        pltpu.make_async_copy(ref, ref, sem).wait()

    y_of = [(y + o) % 4 for o in ORDER]
    small = []
    for n, (src, dst) in enumerate(((sync_h, sync_v), (vrow_h, vrow_v), (se_h, se_v), (lr_h, lr_s))):
        small.append(pltpu.make_async_copy(src, dst, ld.at[n]))
    small[0].start()
    for i in range(4):
        rows = rows_at(y_of[i] * 64, 64, 64)
        for src, dst in ((mom_h, mom_b), (we_h, we_b), (g_h, g_b)):
            pltpu.make_async_copy(src.at[rows], dst.at[rows], ld.at[4 + i]).start()
    for copy in small[1:]:
        copy.start()

    def dev(xx, yy, zz, cc):
        return ((yy * 8 + zz) * 2 + cc, xx)

    def plane(p):
        return (x + p[0]) % 4, (y + p[1]) % 4

    def to_plane(p):
        xx, yy = plane(p)
        return dev(xx, yy, z, c)

    def to_z(k):
        return dev(x, y, (z + k) % 8, c)

    partner = dev(x, y, z, 1 - c)

    def send(src, dst, ssem, rsem, device):
        pltpu.make_async_remote_copy(
            src_ref=src, dst_ref=dst, send_sem=ssem, recv_sem=rsem,
            device_id=device, device_id_type=pl.DeviceIdType.MESH,
        ).start()

    barrier = pltpu.get_barrier_semaphore()
    peers = [to_z(k) for k in FAR_FIRST] + [to_plane(p) for p in PLANE] + [partner]
    for peer in peers:
        pl.semaphore_signal(barrier, inc=1, device_id=peer, device_id_type=pl.DeviceIdType.MESH)

    diagonal = lax.broadcasted_iota(jnp.int32, (128, 128), 0) == lax.broadcasted_iota(jnp.int32, (128, 128), 1)

    def spread(source, mask):
        for k in range(2):
            line = jnp.where(source[k : k + 1, :] == 1, 1.0, 0.0).astype(F32)
            column = jnp.sum(jnp.where(diagonal, jnp.broadcast_to(line, (128, 128)), 0.0), axis=1, keepdims=True)
            mask[pl.ds(k * 128, 128), :] = jnp.broadcast_to(column, (128, 128))

    small[0].wait()
    spread(sync_v, smask)

    for i in range(4):
        drain(mom_b.at[pl.ds(0, 160)], ld.at[4 + i])

        def rows32(n, carry, i=i):
            rows = rows_at(y_of[i] * 64 + n * 32, 32, 32)
            moment = BETA_ONE * mom_b[rows, :] + (1.0 - BETA_ONE) * g_b[rows, :].astype(F32)
            nmom[rows, :] = moment
            error = we_b[rows, :]
            comp = moment + error
            scale = jnp.sum(jnp.abs(comp), axis=1, keepdims=True) * (1.0 / D) + EPS_SCALE
            packed = jnp.minimum(jnp.maximum(4.0 * comp, -scale), scale)
            on = smask[rows, :][:, :1] > 0.5
            terms = jnp.where(on, packed, 0.0)
            nwe[rows, :] = jnp.where(on, comp - packed, error)
            for sub in range(8):
                zz = n * 4 + sub // 2
                half = sub % 2
                for j in range(8):
                    value = terms[sub * 4 : sub * 4 + 4, j * 128 : j * 128 + 128]
                    if j < 6:
                        part_a[pl.ds(half * 768 + y_of[i] * 48 + j * 8 + zz, 4, stride=192), :] = value
                    else:
                        part_b[pl.ds(half * 256 + zz * 32 + y_of[i] * 2 + j - 6, 4, stride=8), :] = value
            return carry

        lax.fori_loop(0, 2, rows32, 0)
    pl.semaphore_wait(barrier, len(peers))
    for i in range(4):
        for xx in range(4):
            at = (xx * 4 + y_of[i]) * 48
            send(
                part_a.at[rows_at((1 - c) * 768 + at, 48)], pair_a.at[rows_at(at, 48)],
                out_sem.at[0], pair_sem.at[i], partner,
            )
    send(part_b.at[rows_at((1 - c) * 256, 256)], pair_b, out_sem.at[0], pair_sem.at[4], partner)
    load_var = pltpu.make_async_copy(var_h, var_b, ld.at[8])
    load_par = pltpu.make_async_copy(par_h, par_b, ld.at[9])

    n = 0
    for i in range(4):
        drain(pair_a.at[pl.ds(0, 192)], pair_sem.at[i])
        for dx in ORDER:
            p = (dx, ORDER[i])
            xx, yy = plane(p)
            at = (xx * 4 + yy) * 48
            here = rows_at(c * 768 + at, 48)
            part_a[here, :] += pair_a[rows_at(at, 48), :]
            if p != (0, 0):
                send(part_a.at[here], in_a.at[n], out_sem.at[1], one.at[0], to_plane(p))
                n += 1
    drain(pair_b, pair_sem.at[4])
    for k in FAR_FIRST + (0,):
        at = ((z + k) % 8) * 32
        here = rows_at(c * 256 + at, 32)
        part_b[here, :] += pair_b[rows_at(at, 32), :]
        if k:
            send(part_b.at[here], in_b.at[k - 1], out_sem.at[1], one.at[1], to_z(k))

    load_var.start()
    load_par.start()

    small[2].wait()
    for j in range(8):
        se_t[j : j + 1, :] = se_v[:, j * 128 : j * 128 + 128]

    drain(in_a, one.at[0])
    total = part_a[rows_at(c * 768 + q * 48, 48), :]
    for n in range(15):
        total = total + in_a[n]
    sum_a[...] = total
    for zz in range(8):
        out_a2[zz, 0:6, :] = sum_a[pl.ds(zz, 6, stride=8), :]
    for k in FAR_FIRST:
        send(out_a2.at[(z + k) % 8], in_a2.at[k - 1], out_sem.at[2], two.at[0], to_z(k))
    drain(in_b, one.at[1])
    here_b = rows_at(c * 256 + z * 32, 32)
    total = part_b[here_b, :]
    for n in range(7):
        total = total + in_b[n]
    for n in range(16):
        out_b2[n] = total[n * 2 : n * 2 + 2, :]
    for n, p in enumerate(PLANE):
        xx, yy = plane(p)
        send(out_b2.at[xx * 4 + yy], in_b2.at[n], out_sem.at[7], two.at[1], to_plane(p))

    small[1].wait()
    small[3].wait()
    spread(vrow_v, vmask)
    rate = lr_s[step_s[0]]
    load_var.wait()
    load_par.wait()

    def rows16v(n, carry):
        rows = rows_at(n * 16, 16, 16)
        g = g_b[rows, :].astype(F32)
        v = var_b[rows, :]
        on = vmask[rows, :][:, :1] > 0.5
        v = jnp.where(on, BETA_TWO * v + (1.0 - BETA_TWO) * g * g, v)
        nvar[rows, :] = v
        npar[rows, :] = rate / (jnp.sqrt(v) + EPS_ADAM)
        return carry

    lax.fori_loop(0, 16, rows16v, 0)

    drain(in_a2, two.at[0])
    total = out_a2[z]
    for n in range(7):
        total = total + in_a2[n]
    row_t[...] = total
    drain(in_b2, two.at[1])
    total = out_b2[q]
    for n in range(15):
        total = total + in_b2[n]
    row_t[6:8, :] = total

    average = row_t[...] * (1.0 / REPLICAS) + se_t[...]
    scale = jnp.sum(jnp.abs(average)) * (1.0 / D) + EPS_SCALE
    synced = jnp.minimum(jnp.maximum(4.0 * average, -scale), scale)
    own_on = smask[pl.ds(y * 64 + z * 8 + c * 4 + x, 1), :]
    squares = jnp.broadcast_to(own_on * (scale * scale), (2, 128))
    row_t[...] = synced
    row_b[0:2, :] = synced[6:8, :]
    row_b[2:4, :] = squares
    for k in FAR_FIRST:
        send(row_t, up_a.at[z], out_sem.at[3], up_one.at[0], to_z(k))
    for p in PLANE:
        send(row_b, up_b.at[q], out_sem.at[8], up_one.at[1], to_plane(p))
    nse_t[...] = jnp.where(own_on > 0.5, average - synced, se_t[...])
    for j in range(8):
        nse[:, j * 128 : j * 128 + 128] = nse_t[j : j + 1, :]
    synced_count = jnp.sum(jnp.where(sync_v[...] == 1, 1.0, 0.0).astype(F32))

    up_a[z] = synced
    up_b[q, 0:2, :] = synced[6:8, :]
    up_b[q, 2:4, :] = squares
    drain(in_a2, up_one.at[0])
    mine_a = rows_at(c * 768 + q * 48, 48)
    for zz in range(8):
        gat_a[pl.ds(c * 768 + q * 48 + zz, 6, stride=8), :] = up_a[zz, 0:6, :]
    for n, group in enumerate(GROUPS_A):
        for m in group:
            send(gat_a.at[mine_a], gat_a.at[mine_a], out_sem.at[4], up_two_a.at[n], to_plane(PLANE[m]))
    send(gat_a.at[mine_a], gat_a.at[mine_a], out_sem.at[5], share_sem, partner)
    drain(up_b.at[pl.ds(0, 15)], up_one.at[1])
    mine_b = rows_at(c * 256 + z * 32, 32)
    part = up_b[0, 2:3, :]
    for n in range(16):
        gat_b[pl.ds(c * 256 + z * 32 + n * 2, 2), :] = up_b[n, 0:2, :]
        if n:
            part = part + up_b[n, 2:3, :]
    s_in[z] = part
    s_mine[...] = part
    for k in FAR_FIRST:
        send(s_mine, s_in.at[z], out_sem.at[6], s_sem.at[0], to_z(k))
    for n, group in enumerate(GROUPS_B):
        for m in group:
            send(gat_b.at[mine_b], gat_b.at[mine_b], out_sem.at[4], up_two_b.at[n], to_z(FAR_FIRST[m]))
    send(gat_b.at[mine_b], gat_b.at[mine_b], out_sem.at[5], share_sem, partner)

    def share_a(group, n):
        drain(gat_a.at[pl.ds(0, 48 * len(group))], up_two_a.at[n])
        for m in group:
            p = PLANE[m]
            ref = gat_a.at[rows_at(c * 768 + (((x + 4 - p[0]) % 4) * 4 + (y + 4 - p[1]) % 4) * 48, 48)]
            send(ref, ref, out_sem.at[5], share_sem, partner)

    def share_b(group, n):
        drain(gat_b.at[pl.ds(0, 32 * len(group))], up_two_b.at[n])
        for m in group:
            ref = gat_b.at[rows_at(c * 256 + ((z + 8 - FAR_FIRST[m]) % 8) * 32, 32)]
            send(ref, ref, out_sem.at[5], share_sem, partner)

    share_a(GROUPS_A[0], 0)
    share_b(GROUPS_B[0], 0)
    share_a(GROUPS_A[1], 1)
    share_b(GROUPS_B[1], 1)
    share_a(GROUPS_A[2], 2)

    drain(s_in.at[pl.ds(0, 7)], s_sem.at[0])
    part = s_in[0]
    for zz in range(1, 8):
        part = part + s_in[zz]
    s_in[8] = part
    send(s_in.at[8], s_other, out_sem.at[6], s_sem.at[1], partner)
    drain(s_other, s_sem.at[1])
    norm_v[...] = jnp.broadcast_to(1.0 / jnp.sqrt((part + s_other[...]) / synced_count), (8, 128))
    drain(gat_a.at[pl.ds(0, 1024)], share_sem)

    drain(gat_a.at[pl.ds(0, 1024)], out_sem.at[0])
    drain(gat_a.at[pl.ds(0, 944)], out_sem.at[1])
    drain(in_a2, out_sem.at[2])
    drain(in_b2, out_sem.at[7])
    drain(in_a2, out_sem.at[3])
    drain(up_b.at[pl.ds(0, 15)], out_sem.at[8])
    drain(gat_a.at[pl.ds(0, 944)], out_sem.at[4])
    drain(gat_a.at[pl.ds(0, 1024)], out_sem.at[5])
    drain(s_in.at[pl.ds(0, 8)], out_sem.at[6])


def finish_kernel(
    gat_a, gat_b, nmom, slope, nvar, nwe, par_b, smask, norm_v, nse,
    par_o, mom_o, var_o, we_o, se_out, value_b, param_b, sems,
):
    copies = []

    def write(src, dst, n):
        copy = pltpu.make_async_copy(src, dst, sems.at[n])
        copy.start()
        copies.append(copy)

    write(nvar, var_o, 0)
    write(nwe, we_o, 1)
    write(nse, se_out, 2)
    norm = norm_v[...]
    for part in range(2):

        def finish(n, carry, part=part):
            y = part * 2 + n // 8
            z = n % 8
            rows = pl.ds(pl.multiple_of(part * 128 + n * 8, 8), 8)
            on = smask[rows, :] > 0.5
            for j in range(8):
                lanes = pl.ds(j * 128, 128)
                if j < 6:
                    at = y * 48 + j * 8 + z
                    halves = [gat_a[pl.ds(half * 768 + at, 4, stride=192), :] for half in range(2)]
                else:
                    at = z * 32 + y * 2 + j - 6
                    halves = [gat_b[pl.ds(half * 256 + at, 4, stride=8), :] for half in range(2)]
                value = jnp.where(on, jnp.concatenate(halves, axis=0), nmom[rows, lanes])
                value_b[rows, lanes] = value
                param_b[rows, lanes] = par_b[rows, lanes] - norm * (slope[rows, lanes] * value)
            return carry

        lax.fori_loop(0, 16, finish, 0)
        rows = pl.ds(part * 128, 128)
        write(value_b.at[rows], mom_o.at[rows], 3 + part)
        write(param_b.at[rows], par_o.at[rows], 5 + part)
    for copy in copies:
        copy.wait()


def on_device(params, momentum, variance, worker_error, grads, server_error, sync_rows, var_rows, step, lr_table):
    in_hbm = lambda v: pltpu.with_memory_space_constraint(v, pltpu.HBM)
    flat = lambda v: in_hbm(v.reshape(ROWS, D))
    hbm = pl.BlockSpec(memory_space=pltpu.HBM)
    vmem = pl.BlockSpec(memory_space=pltpu.VMEM)
    full = jax.ShapeDtypeStruct((ROWS, D), F32)
    dma = pltpu.SemaphoreType.DMA
    one = jax.ShapeDtypeStruct((1, D), F32)
    middle = pl.pallas_call(
        kernel,
        out_shape=(
            jax.ShapeDtypeStruct((1536, 128), F32), jax.ShapeDtypeStruct((512, 128), F32),
            full, full, full, full, full,
            jax.ShapeDtypeStruct((ROWS, 128), F32), jax.ShapeDtypeStruct((8, 128), F32), one,
        ),
        in_specs=[hbm] * 9 + [pl.BlockSpec(memory_space=pltpu.SMEM)],
        out_specs=(vmem,) * 10,
        scratch_shapes=[
            pltpu.VMEM((ROWS, D), F32),
            pltpu.VMEM((ROWS, D), F32),
            pltpu.VMEM((ROWS, D), jnp.bfloat16),
            pltpu.VMEM((ROWS, D), F32),
            pltpu.VMEM((ROWS, 128), F32),
            pltpu.VMEM((1, D), F32),
            pltpu.VMEM((2, 128), jnp.int32),
            pltpu.VMEM((2, 128), jnp.int32),
            pltpu.SMEM((1024,), F32),
            pltpu.VMEM((1536, 128), F32),
            pltpu.VMEM((512, 128), F32),
            pltpu.VMEM((768, 128), F32),
            pltpu.VMEM((256, 128), F32),
            pltpu.VMEM((15, 48, 128), F32),
            pltpu.VMEM((7, 32, 128), F32),
            pltpu.VMEM((48, 128), F32),
            pltpu.VMEM((8, 8, 128), F32),
            pltpu.VMEM((7, 8, 128), F32),
            pltpu.VMEM((16, 2, 128), F32),
            pltpu.VMEM((15, 2, 128), F32),
            pltpu.VMEM((8, 128), F32),
            pltpu.VMEM((4, 128), F32),
            pltpu.VMEM((8, 128), F32),
            pltpu.VMEM((8, 128), F32),
            pltpu.VMEM((8, 8, 128), F32),
            pltpu.VMEM((16, 4, 128), F32),
            pltpu.VMEM((9, 1, 128), F32),
            pltpu.VMEM((1, 128), F32),
            pltpu.VMEM((1, 128), F32),
            dma((10,)), dma((9,)), dma((5,)), dma((2,)), dma((2,)), dma((2,)), dma((2,)),
            dma((3,)), dma((2,)), dma,
        ],
        compiler_params=pltpu.CompilerParams(
            collective_id=0, has_side_effects=True, vmem_limit_bytes=40 * 1024 * 1024
        ),
        name="momentum_exchange",
    )(
        flat(momentum), flat(worker_error), flat(grads), flat(variance), flat(params),
        in_hbm(server_error), in_hbm(sync_rows.reshape(2, 128)), in_hbm(var_rows.reshape(2, 128)),
        in_hbm(lr_table), step,
    )
    outs = pl.pallas_call(
        finish_kernel,
        out_shape=(full, full, full, full, one),
        in_specs=[vmem] * 10,
        out_specs=(hbm,) * 5,
        scratch_shapes=[pltpu.VMEM((ROWS, D), F32), pltpu.VMEM((ROWS, D), F32), dma((7,))],
        compiler_params=pltpu.CompilerParams(vmem_limit_bytes=24 * 1024 * 1024),
        name="update_and_write",
    )(*middle)
    back = lambda v: v.reshape(1, 1, ROWS, D)
    return tuple(back(v) for v in outs[:4]) + (outs[4],)


def solution(mesh):
    big = P("dp", "grp", None, None)
    return jax.shard_map(
        on_device,
        mesh=mesh,
        in_specs=(big,) * 5 + (P(("dp", "grp"), None), P(), P(), P(), P()),
        out_specs=(big,) * 4 + (P(("dp", "grp"), None),),
        check_vma=False,
    )
```

```python
import jax
import jax.numpy as jnp
from jax import lax
from jax.experimental import pallas as pl
from jax.experimental.pallas import tpu as pltpu
from jax.sharding import PartitionSpec as P

BETA_ONE = 0.9
BETA_TWO = 0.95
EPS_SCALE = 1e-06
EPS_ADAM = 1e-08
D = 1024
ROWS = 256
REPLICAS = 256
F32 = jnp.float32
ORDER = (2, 1, 3, 0)
PLANE = [(i, j) for j in ORDER for i in ORDER if (i, j) != (0, 0)]
FAR_FIRST = (4, 3, 5, 2, 6, 1, 7)
GROUPS_A = [range(0, 8), range(8, 15)]
GROUPS_B = [range(0, 7)]


def kernel(
    mom_h, we_h, g_h, var_h, par_h, se_h, sync_h, vrow_h, lr_h, step_s,
    gat_a, gat_b, nmom, npar, nvar, nwe, par_b, smask, norm_v, nse,
    mom_b, we_b, g_b, var_b, vmask, se_v, sync_v, vrow_v, lr_s,
    part_a, part_b, pair_a, pair_b, in_a, in_b, sum_a, out_a2, in_a2, out_b2, in_b2, row_t, row_b, se_t, nse_t,
    up_a, up_b, s_in, s_mine, s_other,
    ld, out_sem, pair_sem, one, two, up_one, s_sem, up_two_a, up_two_b, share_sem,
):
    dp = lax.axis_index("dp")
    x = lax.axis_index("grp")
    c = dp % 2
    z = (dp // 2) % 8
    y = dp // 16
    q = x * 4 + y

    def rows_at(start, size, multiple=8):
        return pl.ds(pl.multiple_of(start, multiple), size)

    def drain(ref, sem):
        pltpu.make_async_copy(ref, ref, sem).wait()

    y_of = [(y + o) % 4 for o in ORDER]
    small = []
    for n, (src, dst) in enumerate(((sync_h, sync_v), (vrow_h, vrow_v), (se_h, se_v), (lr_h, lr_s))):
        small.append(pltpu.make_async_copy(src, dst, ld.at[n]))
    small[0].start()
    for i in range(4):
        rows = rows_at(y_of[i] * 64, 64, 64)
        for src, dst in ((mom_h, mom_b), (we_h, we_b), (g_h, g_b)):
            pltpu.make_async_copy(src.at[rows], dst.at[rows], ld.at[4 + i]).start()
    for copy in small[1:]:
        copy.start()

    def dev(xx, yy, zz, cc):
        return ((yy * 8 + zz) * 2 + cc, xx)

    def plane(p):
        return (x + p[0]) % 4, (y + p[1]) % 4

    def to_plane(p):
        xx, yy = plane(p)
        return dev(xx, yy, z, c)

    def to_z(k):
        return dev(x, y, (z + k) % 8, c)

    partner = dev(x, y, z, 1 - c)

    def send(src, dst, ssem, rsem, device):
        pltpu.make_async_remote_copy(
            src_ref=src, dst_ref=dst, send_sem=ssem, recv_sem=rsem,
            device_id=device, device_id_type=pl.DeviceIdType.MESH,
        ).start()

    barrier = pltpu.get_barrier_semaphore()
    peers = [to_z(k) for k in FAR_FIRST] + [to_plane(p) for p in PLANE] + [partner]
    for peer in peers:
        pl.semaphore_signal(barrier, inc=1, device_id=peer, device_id_type=pl.DeviceIdType.MESH)

    diagonal = lax.broadcasted_iota(jnp.int32, (128, 128), 0) == lax.broadcasted_iota(jnp.int32, (128, 128), 1)

    def spread(source, mask):
        for k in range(2):
            line = jnp.where(source[k : k + 1, :] == 1, 1.0, 0.0).astype(F32)
            column = jnp.sum(jnp.where(diagonal, jnp.broadcast_to(line, (128, 128)), 0.0), axis=1, keepdims=True)
            mask[pl.ds(k * 128, 128), :] = jnp.broadcast_to(column, (128, 128))

    small[0].wait()
    spread(sync_v, smask)

    for i in range(4):
        drain(mom_b.at[pl.ds(0, 160)], ld.at[4 + i])

        def rows32(n, carry, i=i):
            rows = rows_at(y_of[i] * 64 + n * 32, 32, 32)
            moment = BETA_ONE * mom_b[rows, :] + (1.0 - BETA_ONE) * g_b[rows, :].astype(F32)
            nmom[rows, :] = moment
            error = we_b[rows, :]
            comp = moment + error
            scale = jnp.sum(jnp.abs(comp), axis=1, keepdims=True) * (1.0 / D) + EPS_SCALE
            packed = jnp.minimum(jnp.maximum(4.0 * comp, -scale), scale)
            on = smask[rows, :][:, :1] > 0.5
            terms = jnp.where(on, packed, 0.0)
            nwe[rows, :] = jnp.where(on, comp - packed, error)
            for sub in range(8):
                zz = n * 4 + sub // 2
                half = sub % 2
                for j in range(8):
                    value = terms[sub * 4 : sub * 4 + 4, j * 128 : j * 128 + 128]
                    if j < 6:
                        part_a[pl.ds(half * 768 + y_of[i] * 48 + j * 8 + zz, 4, stride=192), :] = value
                    else:
                        part_b[pl.ds(half * 256 + zz * 32 + y_of[i] * 2 + j - 6, 4, stride=8), :] = value
            return carry

        lax.fori_loop(0, 2, rows32, 0)
    pl.semaphore_wait(barrier, len(peers))
    for i in range(4):
        for xx in range(4):
            at = (xx * 4 + y_of[i]) * 48
            send(
                part_a.at[rows_at((1 - c) * 768 + at, 48)], pair_a.at[rows_at(at, 48)],
                out_sem.at[0], pair_sem.at[i], partner,
            )
    send(part_b.at[rows_at((1 - c) * 256, 256)], pair_b, out_sem.at[0], pair_sem.at[4], partner)
    load_var = pltpu.make_async_copy(var_h, var_b, ld.at[8])
    load_par = pltpu.make_async_copy(par_h, par_b, ld.at[9])

    n = 0
    for i in range(4):
        drain(pair_a.at[pl.ds(0, 192)], pair_sem.at[i])
        for dx in ORDER:
            p = (dx, ORDER[i])
            xx, yy = plane(p)
            at = (xx * 4 + yy) * 48
            here = rows_at(c * 768 + at, 48)
            part_a[here, :] += pair_a[rows_at(at, 48), :]
            if p != (0, 0):
                send(part_a.at[here], in_a.at[n], out_sem.at[1], one.at[0], to_plane(p))
                n += 1
    drain(pair_b, pair_sem.at[4])
    for k in FAR_FIRST + (0,):
        at = ((z + k) % 8) * 32
        here = rows_at(c * 256 + at, 32)
        part_b[here, :] += pair_b[rows_at(at, 32), :]
        if k:
            send(part_b.at[here], in_b.at[k - 1], out_sem.at[1], one.at[1], to_z(k))

    load_var.start()
    load_par.start()

    small[2].wait()
    for j in range(8):
        se_t[j : j + 1, :] = se_v[:, j * 128 : j * 128 + 128]

    drain(in_a, one.at[0])
    total = part_a[rows_at(c * 768 + q * 48, 48), :]
    for n in range(15):
        total = total + in_a[n]
    sum_a[...] = total
    for zz in range(8):
        out_a2[zz, 0:6, :] = sum_a[pl.ds(zz, 6, stride=8), :]
    for k in FAR_FIRST:
        send(out_a2.at[(z + k) % 8], in_a2.at[k - 1], out_sem.at[2], two.at[0], to_z(k))
    drain(in_b, one.at[1])
    here_b = rows_at(c * 256 + z * 32, 32)
    total = part_b[here_b, :]
    for n in range(7):
        total = total + in_b[n]
    for n in range(16):
        out_b2[n] = total[n * 2 : n * 2 + 2, :]
    for n, p in enumerate(PLANE):
        xx, yy = plane(p)
        send(out_b2.at[xx * 4 + yy], in_b2.at[n], out_sem.at[7], two.at[1], to_plane(p))

    small[1].wait()
    small[3].wait()
    spread(vrow_v, vmask)
    rate = lr_s[step_s[0]]
    load_var.wait()
    load_par.wait()

    def rows16v(n, carry):
        rows = rows_at(n * 16, 16, 16)
        g = g_b[rows, :].astype(F32)
        v = var_b[rows, :]
        on = vmask[rows, :][:, :1] > 0.5
        v = jnp.where(on, BETA_TWO * v + (1.0 - BETA_TWO) * g * g, v)
        nvar[rows, :] = v
        npar[rows, :] = rate / (jnp.sqrt(v) + EPS_ADAM)
        return carry

    lax.fori_loop(0, 16, rows16v, 0)

    drain(in_a2, two.at[0])
    total = out_a2[z]
    for n in range(7):
        total = total + in_a2[n]
    row_t[...] = total
    drain(in_b2, two.at[1])
    total = out_b2[q]
    for n in range(15):
        total = total + in_b2[n]
    row_t[6:8, :] = total

    average = row_t[...] * (1.0 / REPLICAS) + se_t[...]
    scale = jnp.sum(jnp.abs(average)) * (1.0 / D) + EPS_SCALE
    synced = jnp.minimum(jnp.maximum(4.0 * average, -scale), scale)
    own_on = smask[pl.ds(y * 64 + z * 8 + c * 4 + x, 1), :]
    squares = jnp.broadcast_to(own_on * (scale * scale), (2, 128))
    row_t[...] = synced
    row_b[0:2, :] = synced[6:8, :]
    row_b[2:4, :] = squares
    for k in FAR_FIRST:
        send(row_t, up_a.at[z], out_sem.at[2], up_one.at[0], to_z(k))
    for p in PLANE:
        send(row_b, up_b.at[q], out_sem.at[3], up_one.at[1], to_plane(p))
    nse_t[...] = jnp.where(own_on > 0.5, average - synced, se_t[...])
    for j in range(8):
        nse[:, j * 128 : j * 128 + 128] = nse_t[j : j + 1, :]
    synced_count = jnp.sum(jnp.where(sync_v[...] == 1, 1.0, 0.0).astype(F32))

    up_a[z] = synced
    up_b[q, 0:2, :] = synced[6:8, :]
    up_b[q, 2:4, :] = squares
    drain(in_a2, up_one.at[0])
    mine_a = rows_at(c * 768 + q * 48, 48)
    for zz in range(8):
        gat_a[pl.ds(c * 768 + q * 48 + zz, 6, stride=8), :] = up_a[zz, 0:6, :]
    for n, group in enumerate(GROUPS_A):
        for m in group:
            send(gat_a.at[mine_a], gat_a.at[mine_a], out_sem.at[4], up_two_a.at[n], to_plane(PLANE[m]))
    send(gat_a.at[mine_a], gat_a.at[mine_a], out_sem.at[5], share_sem, partner)
    drain(up_b.at[pl.ds(0, 15)], up_one.at[1])
    mine_b = rows_at(c * 256 + z * 32, 32)
    part = up_b[0, 2:3, :]
    for n in range(16):
        gat_b[pl.ds(c * 256 + z * 32 + n * 2, 2), :] = up_b[n, 0:2, :]
        if n:
            part = part + up_b[n, 2:3, :]
    s_in[z] = part
    s_mine[...] = part
    for k in FAR_FIRST:
        send(s_mine, s_in.at[z], out_sem.at[6], s_sem.at[0], to_z(k))
    for n, group in enumerate(GROUPS_B):
        for m in group:
            send(gat_b.at[mine_b], gat_b.at[mine_b], out_sem.at[4], up_two_b.at[n], to_z(FAR_FIRST[m]))
    send(gat_b.at[mine_b], gat_b.at[mine_b], out_sem.at[5], share_sem, partner)

    def share_a(group, n):
        drain(gat_a.at[pl.ds(0, 48 * len(group))], up_two_a.at[n])
        for m in group:
            p = PLANE[m]
            ref = gat_a.at[rows_at(c * 768 + (((x + 4 - p[0]) % 4) * 4 + (y + 4 - p[1]) % 4) * 48, 48)]
            send(ref, ref, out_sem.at[5], share_sem, partner)

    def share_b(group, n):
        drain(gat_b.at[pl.ds(0, 32 * len(group))], up_two_b.at[n])
        for m in group:
            ref = gat_b.at[rows_at(c * 256 + ((z + 8 - FAR_FIRST[m]) % 8) * 32, 32)]
            send(ref, ref, out_sem.at[5], share_sem, partner)

    share_a(GROUPS_A[0], 0)
    share_b(GROUPS_B[0], 0)
    share_a(GROUPS_A[1], 1)

    drain(s_in.at[pl.ds(0, 7)], s_sem.at[0])
    part = s_in[0]
    for zz in range(1, 8):
        part = part + s_in[zz]
    s_in[8] = part
    send(s_in.at[8], s_other, out_sem.at[6], s_sem.at[1], partner)
    drain(s_other, s_sem.at[1])
    norm_v[...] = jnp.broadcast_to(1.0 / jnp.sqrt((part + s_other[...]) / synced_count), (8, 128))
    drain(gat_a.at[pl.ds(0, 1024)], share_sem)

    drain(gat_a.at[pl.ds(0, 1024)], out_sem.at[0])
    drain(gat_a.at[pl.ds(0, 944)], out_sem.at[1])
    drain(gat_a.at[pl.ds(0, 112)], out_sem.at[2])
    drain(in_b2, out_sem.at[7])
    drain(up_b.at[pl.ds(0, 15)], out_sem.at[3])
    drain(gat_a.at[pl.ds(0, 944)], out_sem.at[4])
    drain(gat_a.at[pl.ds(0, 1024)], out_sem.at[5])
    drain(s_in.at[pl.ds(0, 8)], out_sem.at[6])


def finish_kernel(
    gat_a, gat_b, nmom, slope, nvar, nwe, par_b, smask, norm_v, nse,
    par_o, mom_o, var_o, we_o, se_out, value_b, param_b, sems,
):
    copies = []

    def write(src, dst, n):
        copy = pltpu.make_async_copy(src, dst, sems.at[n])
        copy.start()
        copies.append(copy)

    write(nvar, var_o, 0)
    write(nwe, we_o, 1)
    write(nse, se_out, 2)
    norm = norm_v[...]
    for part in range(2):

        def finish(n, carry, part=part):
            y = part * 2 + n // 8
            z = n % 8
            rows = pl.ds(pl.multiple_of(part * 128 + n * 8, 8), 8)
            on = smask[rows, :] > 0.5
            for j in range(8):
                lanes = pl.ds(j * 128, 128)
                if j < 6:
                    at = y * 48 + j * 8 + z
                    halves = [gat_a[pl.ds(half * 768 + at, 4, stride=192), :] for half in range(2)]
                else:
                    at = z * 32 + y * 2 + j - 6
                    halves = [gat_b[pl.ds(half * 256 + at, 4, stride=8), :] for half in range(2)]
                value = jnp.where(on, jnp.concatenate(halves, axis=0), nmom[rows, lanes])
                value_b[rows, lanes] = value
                param_b[rows, lanes] = par_b[rows, lanes] - norm * (slope[rows, lanes] * value)
            return carry

        lax.fori_loop(0, 16, finish, 0)
        rows = pl.ds(part * 128, 128)
        write(value_b.at[rows], mom_o.at[rows], 3 + part)
        write(param_b.at[rows], par_o.at[rows], 5 + part)
    for copy in copies:
        copy.wait()


def on_device(params, momentum, variance, worker_error, grads, server_error, sync_rows, var_rows, step, lr_table):
    in_hbm = lambda v: pltpu.with_memory_space_constraint(v, pltpu.HBM)
    flat = lambda v: in_hbm(v.reshape(ROWS, D))
    hbm = pl.BlockSpec(memory_space=pltpu.HBM)
    vmem = pl.BlockSpec(memory_space=pltpu.VMEM)
    full = jax.ShapeDtypeStruct((ROWS, D), F32)
    dma = pltpu.SemaphoreType.DMA
    one = jax.ShapeDtypeStruct((1, D), F32)
    middle = pl.pallas_call(
        kernel,
        out_shape=(
            jax.ShapeDtypeStruct((1536, 128), F32), jax.ShapeDtypeStruct((512, 128), F32),
            full, full, full, full, full,
            jax.ShapeDtypeStruct((ROWS, 128), F32), jax.ShapeDtypeStruct((8, 128), F32), one,
        ),
        in_specs=[hbm] * 9 + [pl.BlockSpec(memory_space=pltpu.SMEM)],
        out_specs=(vmem,) * 10,
        scratch_shapes=[
            pltpu.VMEM((ROWS, D), F32),
            pltpu.VMEM((ROWS, D), F32),
            pltpu.VMEM((ROWS, D), jnp.bfloat16),
            pltpu.VMEM((ROWS, D), F32),
            pltpu.VMEM((ROWS, 128), F32),
            pltpu.VMEM((1, D), F32),
            pltpu.VMEM((2, 128), jnp.int32),
            pltpu.VMEM((2, 128), jnp.int32),
            pltpu.SMEM((1024,), F32),
            pltpu.VMEM((1536, 128), F32),
            pltpu.VMEM((512, 128), F32),
            pltpu.VMEM((768, 128), F32),
            pltpu.VMEM((256, 128), F32),
            pltpu.VMEM((15, 48, 128), F32),
            pltpu.VMEM((7, 32, 128), F32),
            pltpu.VMEM((48, 128), F32),
            pltpu.VMEM((8, 8, 128), F32),
            pltpu.VMEM((7, 8, 128), F32),
            pltpu.VMEM((16, 2, 128), F32),
            pltpu.VMEM((15, 2, 128), F32),
            pltpu.VMEM((8, 128), F32),
            pltpu.VMEM((4, 128), F32),
            pltpu.VMEM((8, 128), F32),
            pltpu.VMEM((8, 128), F32),
            pltpu.VMEM((8, 8, 128), F32),
            pltpu.VMEM((16, 4, 128), F32),
            pltpu.VMEM((9, 1, 128), F32),
            pltpu.VMEM((1, 128), F32),
            pltpu.VMEM((1, 128), F32),
            dma((10,)), dma((8,)), dma((5,)), dma((2,)), dma((2,)), dma((2,)), dma((2,)),
            dma((2,)), dma((1,)), dma,
        ],
        compiler_params=pltpu.CompilerParams(
            collective_id=0, has_side_effects=True, vmem_limit_bytes=40 * 1024 * 1024
        ),
        name="momentum_exchange",
    )(
        flat(momentum), flat(worker_error), flat(grads), flat(variance), flat(params),
        in_hbm(server_error), in_hbm(sync_rows.reshape(2, 128)), in_hbm(var_rows.reshape(2, 128)),
        in_hbm(lr_table), step,
    )
    outs = pl.pallas_call(
        finish_kernel,
        out_shape=(full, full, full, full, one),
        in_specs=[vmem] * 10,
        out_specs=(hbm,) * 5,
        scratch_shapes=[pltpu.VMEM((ROWS, D), F32), pltpu.VMEM((ROWS, D), F32), dma((7,))],
        compiler_params=pltpu.CompilerParams(vmem_limit_bytes=24 * 1024 * 1024),
        name="update_and_write",
    )(*middle)
    back = lambda v: v.reshape(1, 1, ROWS, D)
    return tuple(back(v) for v in outs[:4]) + (outs[4],)


def solution(mesh):
    big = P("dp", "grp", None, None)
    return jax.shard_map(
        on_device,
        mesh=mesh,
        in_specs=(big,) * 5 + (P(("dp", "grp"), None), P(), P(), P(), P()),
        out_specs=(big,) * 4 + (P(("dp", "grp"), None),),
        check_vma=False,
    )
```
